512 devices in a mesh: tm: 32 (over y, x), blk: 16 (over z, core).
Axes of the slice: x: 4, y: 8, z: 8, core: 2. Of those that a mesh axis runs over, the one named last changes fastest.
Arguments:
- panel_strip: bfloat16 [32, 8192, 2304], P('tm', 'blk'), may hold values from -6 to 6
- pivot_inverses: bfloat16 [32, 2, 256, 256], P('tm'), may hold values from -0.0234375 to 0.0234375
- coupling: float32 [32, 256, 256], P('tm'), may hold values from -0.375 to 0.375
- pivot_nodes: int32 [3, 256], replicated, may hold values from 0 to 8191, as said below
Outputs:
- trailing: bfloat16 [32, 8192, 1792], P('tm', 'blk')
- reduced: float32 [32, 256, 256], P('tm')
The draws below stay inside these ranges and needn't reach their ends.
Inputs may be any that keep to these rules, and one draw needn't show every extreme that they name: `pivot_nodes`: entry j of every row is a node of the range [(j // 16) * 512, (j // 16 + 1) * 512); all 768 entries differ.
All inputs are finite; a program needn't handle non-finite values.
Results may differ from the reference program's by a relative error of at most 0.0068.
Values may be sent and summed in bfloat16 or wider, within the bound.
No kernel may reach another device: no remote copies, remote signals or barrier semaphores. Data moves between devices by JAX's collectives and lax.ppermute only.
A program may use at most 128 MiB of HBM per device.

```python
import jax
import jax.numpy as jnp
from jax import lax

M = 8192
W = 256
PARTS_SIZE = 32
ROWS_DEV = 512
PB = 16
NCOL = 2304


def draw_pivot_nodes(key, part):
    blocks = M // ROWS_DEV
    keys = jax.random.split(key, blocks)

    def choose(single_key):
        return jax.random.permutation(single_key, ROWS_DEV)[:3 * PB]
    chosen = jax.vmap(choose)(keys).astype(jnp.int32) + (jnp.arange(blocks, dtype=jnp.int32) * ROWS_DEV)[:, None]
    return jnp.transpose(chosen.reshape(blocks, 3, PB), (1, 0, 2)).reshape(3, W).astype(jnp.int32)


def block_levels(key, extent, shards, least, top_value):
    factor_of = 1.0
    for dim, parts in shards:
        heights = jax.random.uniform(jax.random.fold_in(jax.random.fold_in(key, 6), dim), (parts,), jnp.float32, least / len(shards), top_value / len(shards))
        factor_of = factor_of * jnp.repeat(jnp.exp(heights), extent[dim] // parts).reshape((-1,) + (1,) * (len(extent) - 1 - dim))
    return factor_of


def gaussian(stream_key, extent, spread, limit, cuts=(), kind=jnp.bfloat16):
    drawn = spread * jax.random.normal(stream_key, extent, jnp.float32)
    if cuts:
        drawn = drawn * block_levels(stream_key, extent, cuts, -0.22, 0.18)
    return jnp.clip(drawn, -limit, limit).astype(kind)


def setup_inputs(seed: int = 0) -> dict:
    key_of = jax.random.split(jax.random.key(seed), 5)
    panel_strip = gaussian(key_of[0], (PARTS_SIZE, M, NCOL), 1.0, 6.0, ((0, 32), (1, 16)))
    pivot_inverses = gaussian(key_of[1], (PARTS_SIZE, 2, W, W), (W * W) ** -0.5, 0.0234375, ((0, 32),))
    coupling = gaussian(key_of[2], (PARTS_SIZE, W, W), (W + W // 16) ** -0.5, 0.375, ((0, 32),), jnp.float32)
    pivot_nodes = draw_pivot_nodes(jax.random.fold_in(key_of[4], 71), 0)
    return {"panel_strip": panel_strip, "pivot_inverses": pivot_inverses, "coupling": coupling, "pivot_nodes": pivot_nodes}


def matmul_high(left, right):
    return jnp.dot(left, right, precision=lax.Precision.HIGHEST, preferred_element_type=jnp.float32)


def reference(panel_strip, pivot_inverses, coupling, pivot_nodes):
    def eliminate(inputs):
        strip_block, inverse_pair = inputs
        panel_width = inverse_pair.shape[-1]
        first_rows = strip_block[pivot_nodes[0], panel_width:]
        factor_one = jnp.dot(strip_block[:, :panel_width], inverse_pair[0], preferred_element_type=jnp.float32).astype(jnp.bfloat16)
        updated = (strip_block[:, panel_width:].astype(jnp.float32) - jnp.dot(factor_one, first_rows, preferred_element_type=jnp.float32)).astype(jnp.bfloat16)
        factor_two = jnp.dot(updated[:, :panel_width], inverse_pair[1], preferred_element_type=jnp.float32).astype(jnp.bfloat16)
        second_rows = updated[pivot_nodes[1], panel_width:]
        trailing = (updated[:, panel_width:].astype(jnp.float32) - jnp.dot(factor_two, second_rows, preferred_element_type=jnp.float32)).astype(jnp.bfloat16)
        boundary_block = trailing[pivot_nodes[2], :panel_width].astype(jnp.float32)
        return trailing, boundary_block

    trailing, boundary = lax.map(eliminate, (panel_strip, pivot_inverses))

    def advance(previous, inputs):
        coupling_here, boundary_here = inputs
        current = matmul_high(matmul_high(coupling_here, previous), coupling_here.T) + boundary_here
        return current, current

    initial = jnp.zeros((W, W), jnp.float32)
    final_state, reduced = lax.scan(advance, initial, (coupling, boundary))
    return trailing, reduced
```

```python
import jax
import jax.numpy as jnp
from jax import lax
from jax.sharding import PartitionSpec as P


def passed_along(x, axis, by):
    count = lax.axis_size(axis)
    return lax.ppermute(x, axis, [(i, i + by) for i in range(count - by)])


def matmul_high(left, right):
    return jnp.dot(left, right, precision=lax.Precision.HIGHEST, preferred_element_type=jnp.float32)


def rounded_dot(left, right):
    return jnp.dot(left, right, preferred_element_type=jnp.float32).astype(jnp.bfloat16)


def reduced_by(block, factor, rows):
    product = jnp.dot(factor, rows, preferred_element_type=jnp.float32)
    return (block.astype(jnp.float32) - product).astype(jnp.bfloat16)


def body(panel_strip, pivot_inverses, coupling, pivot_nodes):
    strip = panel_strip[0]
    first_inverse, second_inverse = pivot_inverses[0, 0], pivot_inverses[0, 1]
    coupling_here = coupling[0]
    w = coupling_here.shape[0]
    rows_here = strip.shape[0]
    per_device = w // lax.axis_size("blk")
    my_index = lax.axis_index("blk")
    local_rows = (
        lax.dynamic_slice_in_dim(pivot_nodes, my_index * per_device, per_device, 1)
        - my_index * rows_here
    ).reshape(-1)
    picker = (
        local_rows[:, None] == lax.broadcasted_iota(jnp.int32, (3 * per_device, rows_here), 1)
    ).astype(jnp.bfloat16)
    picked = rounded_dot(picker, strip)
    rows_one, rows_two, rows_edge = (
        picked[i * per_device:(i + 1) * per_device] for i in range(3)
    )

    near = lax.all_gather(
        jnp.concatenate(
            [rows_one[:, w:3 * w], rows_two[:, :w], rows_two[:, 2 * w:3 * w], rows_edge[:, :3 * w]], 1
        ),
        "blk", axis=0, tiled=True,
    )
    far = lax.all_gather(
        jnp.concatenate([rows_one[:, 3 * w:], rows_two[:, 3 * w:]], 1), "blk", axis=0, tiled=True
    )
    one_next, one_edge = near[:, :w], near[:, w:2 * w]
    two_panel, two_edge = near[:, 2 * w:3 * w], near[:, 3 * w:4 * w]
    edge = near[:, 4 * w:]

    factor_at_two = rounded_dot(two_panel, first_inverse)
    factor_at_edge = rounded_dot(edge[:, :w], first_inverse)
    second_edge = reduced_by(two_edge, factor_at_two, one_edge)
    edge_updated = reduced_by(edge[:, w:], factor_at_edge, near[:, :2 * w])
    edge_factor_two = rounded_dot(edge_updated[:, :w], second_inverse)
    boundary = reduced_by(edge_updated[:, w:], edge_factor_two, second_edge)

    count = lax.axis_size("tm")
    span = coupling_here
    current = boundary.astype(jnp.float32)
    step = 1
    while step < count:
        incoming = passed_along(current.astype(jnp.bfloat16), "tm", step).astype(jnp.float32)
        current = matmul_high(matmul_high(span, incoming), span.T) + current
        if 2 * step < count:
            span = matmul_high(span, passed_along(span, "tm", step))
        step *= 2
    reduced = current

    factor_one = rounded_dot(strip[:, :w], first_inverse)
    next_panel = reduced_by(strip[:, w:2 * w], factor_one, one_next)
    factor_two = rounded_dot(next_panel, second_inverse)
    far_one, far_two = jnp.split(far, 2, 1)
    second_far = reduced_by(far_two, factor_at_two, far_one)
    one_rows = jnp.concatenate([one_edge, far_one], 1)
    two_rows = jnp.concatenate([second_edge, second_far], 1)
    updated = reduced_by(strip[:, 2 * w:], factor_one, one_rows)
    trailing = reduced_by(updated, factor_two, two_rows)
    return (trailing[None], reduced[None])


def solution(mesh):
    placed = (P("tm", "blk", None), P("tm", None, None, None), P("tm", None, None), P())
    return jax.shard_map(
        body,
        mesh=mesh,
        in_specs=placed,
        out_specs=(P("tm", "blk", None), P("tm", None, None)),
        check_vma=False,
    )
```

```python
import jax
import jax.numpy as jnp
from jax import lax
from jax.experimental import pallas as pl
from jax.experimental.pallas import tpu as pltpu
from jax.sharding import PartitionSpec as P

BF16 = jnp.bfloat16
F32 = jnp.float32


def passed_along(x, axis, by):
    count = lax.axis_size(axis)
    return lax.ppermute(x, axis, [(i, i + by) for i in range(count - by)])


def matmul_high(left, right):
    return jnp.dot(left, right, precision=lax.Precision.HIGHEST, preferred_element_type=F32)


def rounded_dot(left, right):
    return jnp.dot(left, right, preferred_element_type=F32).astype(BF16)


def reduced_by(block, factor, rows):
    product = jnp.dot(factor, rows, preferred_element_type=F32)
    return (block.astype(F32) - product).astype(BF16)


def pick_kernel(w, per, chunks, nodes_ref, strip_hbm, near_ref, far_ref, strip_ref, sems):
    rows = strip_ref.shape[0]
    cols = strip_ref.shape[1] // chunks

    def part(i):
        at = pl.ds(i * cols, cols)
        return pltpu.make_async_copy(strip_hbm.at[:, at], strip_ref.at[:, at], sems.at[i])

    for i in range(chunks):
        part(i).start()
    me = lax.axis_index("blk")
    at_row = lax.broadcasted_iota(jnp.int32, (3 * per, rows), 0)
    at_lane = lax.broadcasted_iota(jnp.int32, (3 * per, rows), 1)
    wanted = jnp.zeros((3 * per, rows), jnp.int32)
    for k in range(3):
        for i in range(per):
            node = nodes_ref[k, me * per + i] - me * rows
            wanted = jnp.where(at_row == k * per + i, node, wanted)
    picker = (wanted == at_lane).astype(F32).astype(BF16)
    far_width = strip_ref.shape[1] - 3 * w
    for i in range(chunks):
        part(i).wait()
        at = pl.ds(i * cols, cols)
        got = jnp.dot(picker, strip_ref[:, at], preferred_element_type=F32).astype(BF16)
        one, two, edge = got[:per], got[per:2 * per], got[2 * per:]
        if i == 0:
            near_ref[:, :2 * w] = one[:, w:]
            near_ref[:, 2 * w:3 * w] = two[:, :w]
            near_ref[:, 3 * w:4 * w] = two[:, 2 * w:]
            near_ref[:, 4 * w:] = edge
        else:
            far_ref[:, (i - 1) * cols:i * cols] = one
            far_ref[:, far_width + (i - 1) * cols:far_width + i * cols] = two


def picked_rows(pivot_nodes, strip, w, per):
    rows, width = strip.shape
    chunks = width // (3 * w)
    return pl.pallas_call(
        lambda *refs: pick_kernel(w, per, chunks, *refs),
        out_shape=(
            jax.ShapeDtypeStruct((per, 7 * w), BF16),
            jax.ShapeDtypeStruct((per, 2 * (width - 3 * w)), BF16),
        ),
        in_specs=[pl.BlockSpec(memory_space=pltpu.SMEM), pl.BlockSpec(memory_space=pl.ANY)],
        out_specs=(pl.BlockSpec(memory_space=pltpu.VMEM), pl.BlockSpec(memory_space=pltpu.VMEM)),
        scratch_shapes=[pltpu.VMEM((rows, width), BF16), pltpu.SemaphoreType.DMA((chunks,))],
        cost_estimate=pl.CostEstimate(
            flops=2 * 3 * per * rows * width, bytes_accessed=2 * rows * width, transcendentals=0
        ),
        name="pick",
    )(pivot_nodes, strip)


def boundary_kernel(w, near_ref, inverse_ref, boundary_ref, factor_ref, second_ref):
    near = near_ref[...]
    one_edge = near[:, w:2 * w]
    edge = near[:, 4 * w:]
    factor_at_two = rounded_dot(near[:, 2 * w:3 * w], inverse_ref[0])
    factor_at_edge = rounded_dot(edge[:, :w], inverse_ref[0])
    updated = reduced_by(edge[:, w:], factor_at_edge, near[:, :2 * w])
    second_edge = reduced_by(near[:, 3 * w:4 * w], factor_at_two, one_edge)
    factor_two = rounded_dot(updated[:, :w], inverse_ref[1])
    boundary_ref[...] = reduced_by(updated[:, w:], factor_two, second_edge)
    factor_ref[...] = factor_at_two
    second_ref[...] = second_edge


def boundary_of(near, inverses):
    w = near.shape[0]
    block = jax.ShapeDtypeStruct((w, w), BF16)
    vmem = pl.BlockSpec(memory_space=pltpu.VMEM)
    return pl.pallas_call(
        lambda *refs: boundary_kernel(w, *refs),
        out_shape=(block, block, block),
        in_specs=[vmem, vmem],
        out_specs=(vmem, vmem, vmem),
        cost_estimate=pl.CostEstimate(flops=14 * w * w * w, bytes_accessed=12 * w * 2 * w, transcendentals=0),
        name="boundary",
    )(near, inverses)


def trailing_kernel(
    w, per, panels_ref, block_ref, inverse_ref, near_ref, factor_ref, second_ref, own_ref, other_ref,
    out_ref, one_ref, two_ref, far_ref,
):
    step = pl.program_id(0)
    half = far_ref.shape[1] // 2

    def finish(one_rows, two_rows):
        updated = reduced_by(block_ref[...], one_ref[...], one_rows)
        out_ref[...] = reduced_by(updated, two_ref[...], two_rows)

    @pl.when(step == 0)
    def _():
        me = lax.axis_index("blk")
        chip, core = me // 2, lax.rem(me, 2)
        chips = far_ref.shape[0] // (2 * per)
        for m, shift in enumerate(chip_shifts(chips)):
            source = 2 * lax.rem(chip + chips - shift, chips)
            for ref, which in ((own_ref, core), (other_ref, 1 - core)):
                at = pl.multiple_of((source + which) * per, per)
                far_ref[pl.ds(at, per), :] = ref[m * per:(m + 1) * per, :]
        one_ref[...] = rounded_dot(panels_ref[:, :w], inverse_ref[0])
        panel = reduced_by(panels_ref[:, w:], one_ref[...], near_ref[:, :w])
        two_ref[...] = rounded_dot(panel, inverse_ref[1])
        finish(near_ref[:, w:], second_ref[...])

    @pl.when(step > 0)
    def _():
        at = pl.multiple_of((step - 1) * w, w)
        one_rows = far_ref[:, pl.ds(at, w)]
        finish(one_rows, reduced_by(far_ref[:, pl.ds(half + at, w)], factor_ref[...], one_rows))


def trailing_of(strip, inverses, near, factor_at_two, second_edge, own, other, per):
    rows, width = strip.shape
    w = near.shape[0]
    fixed = lambda i: (0, 0)
    return pl.pallas_call(
        lambda *refs: trailing_kernel(w, per, *refs),
        out_shape=jax.ShapeDtypeStruct((rows, width - 2 * w), BF16),
        grid=(width // w - 2,),
        in_specs=[
            pl.BlockSpec((rows, 2 * w), fixed),
            pl.BlockSpec((rows, w), lambda i: (0, i + 2)),
            pl.BlockSpec((2, w, w), lambda i: (0, 0, 0)),
            pl.BlockSpec((w, 2 * w), fixed),
            pl.BlockSpec((w, w), fixed),
            pl.BlockSpec((w, w), fixed),
            pl.BlockSpec(own.shape, fixed),
            pl.BlockSpec(own.shape, fixed),
        ],
        out_specs=pl.BlockSpec((rows, w), lambda i: (0, i)),
        scratch_shapes=[
            pltpu.VMEM((rows, w), BF16),
            pltpu.VMEM((rows, w), BF16),
            pltpu.VMEM((w, own.shape[1]), BF16),
        ],
        cost_estimate=pl.CostEstimate(
            flops=4 * rows * w * width, bytes_accessed=4 * rows * width + 4 * w * width, transcendentals=0
        ),
        name="trailing",
    )(strip, strip, inverses, near, factor_at_two, second_edge, own, other)


def chip_shifts(chips):
    return [0] + [s for by in range(1, chips // 2) for s in (by, chips - by)] + [chips // 2]


def body(panel_strip, pivot_inverses, coupling, pivot_nodes):
    strip = panel_strip[0]
    inverses = pivot_inverses[0]
    span = coupling[0]
    w = span.shape[0]
    blocks = lax.axis_size("blk")
    per = w // blocks

    back_one, back_two, back_three = (passed_along(span, "tm", by) for by in (1, 2, 3))

    near_here, far_here = picked_rows(pivot_nodes, strip, w, per)
    near = lax.all_gather(near_here, "blk", axis=0, tiled=True)
    boundary, factor_at_two, second_edge = boundary_of(near, inverses)
    back_one, back_two, back_three, boundary, far_here = lax.optimization_barrier(
        (back_one, back_two, back_three, boundary, far_here)
    )

    shifts = chip_shifts(blocks // 2)
    far_from = {0: far_here}

    def send_far(gate, which):
        gate, block = lax.optimization_barrier((gate, far_here))
        for shift in which:
            pairs = [(i, (i + 2 * shift) % blocks) for i in range(blocks)]
            far_from[shift] = lax.ppermute(block, "blk", pairs)
        return gate

    def arrived(value, which):
        value, *blocks_in = lax.optimization_barrier((value, *(far_from[s] for s in which)))
        far_from.update(zip(which, blocks_in))
        return value

    def advance(current, incoming, reach):
        return matmul_high(matmul_high(reach, incoming.astype(F32)), reach.T) + current

    groups = [shifts[6:], shifts[3:6], shifts[1:3]]

    incoming = passed_along(boundary, "tm", 1)
    span_two = send_far(matmul_high(span, back_one), groups[0])
    span_four = matmul_high(span_two, matmul_high(back_two, back_three))
    current = advance(boundary.astype(F32), incoming, span)

    current, span_four = lax.optimization_barrier((current, span_four))
    incoming = passed_along(current.astype(BF16), "tm", 2)
    current = send_far(current, groups[1])
    span_eight = matmul_high(span_four, passed_along(span_four, "tm", 4))
    incoming = arrived(incoming, groups[0])
    current = advance(current, incoming, span_two)

    current, span_eight = lax.optimization_barrier((current, span_eight))
    incoming = passed_along(current.astype(BF16), "tm", 4)
    current = send_far(current, groups[2])
    incoming = arrived(incoming, groups[1])
    current = advance(current, incoming, span_four)

    current = arrived(current, groups[2])
    incoming = passed_along(current.astype(BF16), "tm", 8)
    own = jnp.concatenate([far_from[s] for s in shifts], 0)
    other = lax.ppermute(own, "blk", [(i, i ^ 1) for i in range(blocks)])
    span_sixteen = matmul_high(span_eight, passed_along(span_eight, "tm", 8))
    incoming, other, span_sixteen = lax.optimization_barrier((incoming, other, span_sixteen))
    current = advance(current, incoming, span_eight)

    current, other = lax.optimization_barrier((current, other))
    incoming = passed_along(current.astype(BF16), "tm", 16)
    trailing = trailing_of(strip, inverses, near, factor_at_two, second_edge, own, other, per)
    incoming, trailing = lax.optimization_barrier((incoming, trailing))
    current = advance(current, incoming, span_sixteen)
    return (trailing[None], current[None])


def solution(mesh):
    placed = (P("tm", "blk", None), P("tm", None, None, None), P("tm", None, None), P())
    return jax.shard_map(
        body,
        mesh=mesh,
        in_specs=placed,
        out_specs=(P("tm", "blk", None), P("tm", None, None)),
        check_vma=False,
    )
```

```python
import jax
import jax.numpy as jnp
from jax import lax
from jax.experimental import pallas as pl
from jax.experimental.pallas import tpu as pltpu
from jax.sharding import PartitionSpec as P

BF16 = jnp.bfloat16
F32 = jnp.float32


def passed_along(x, axis, by):
    count = lax.axis_size(axis)
    return lax.ppermute(x, axis, [(i, i + by) for i in range(count - by)])


def matmul_high(left, right):
    return jnp.dot(left, right, precision=lax.Precision.HIGHEST, preferred_element_type=F32)


def rounded_dot(left, right):
    return jnp.dot(left, right, preferred_element_type=F32).astype(BF16)


def reduced_by(block, factor, rows):
    product = jnp.dot(factor, rows, preferred_element_type=F32)
    return (block.astype(F32) - product).astype(BF16)


def pick_kernel(w, per, chunks, nodes_ref, strip_hbm, near_ref, far_ref, strip_ref, sems):
    rows = strip_ref.shape[0]
    cols = strip_ref.shape[1] // chunks

    def part(i):
        at = pl.ds(i * cols, cols)
        return pltpu.make_async_copy(strip_hbm.at[:, at], strip_ref.at[:, at], sems.at[i])

    for i in range(chunks):
        part(i).start()
    me = lax.axis_index("blk")
    lanes = 128
    at_row = lax.broadcasted_iota(jnp.int32, (3 * per, lanes), 0)
    at_lane = lax.broadcasted_iota(jnp.int32, (3 * per, lanes), 1)
    wanted = jnp.zeros((3 * per, lanes), jnp.int32)
    for k in range(3):
        for i in range(per):
            wanted = jnp.where(at_row == k * per + i, nodes_ref[k, me * per + i] - me * rows, wanted)
    picker = jnp.concatenate(
        [(wanted == at_lane + first).astype(F32).astype(BF16) for first in range(0, rows, lanes)], 1
    )
    far_width = strip_ref.shape[1] - 3 * w
    for i in range(chunks):
        part(i).wait()
        at = pl.ds(i * cols, cols)
        got = jnp.dot(picker, strip_ref[:, at], preferred_element_type=F32).astype(BF16)
        one, two, edge = got[:per], got[per:2 * per], got[2 * per:]
        if i == 0:
            near_ref[:, :2 * w] = one[:, w:]
            near_ref[:, 2 * w:3 * w] = two[:, :w]
            near_ref[:, 3 * w:4 * w] = two[:, 2 * w:]
            near_ref[:, 4 * w:] = edge
        else:
            far_ref[:, (i - 1) * cols:i * cols] = one
            far_ref[:, far_width + (i - 1) * cols:far_width + i * cols] = two


def picked_rows(pivot_nodes, strip, w, per):
    rows, width = strip.shape
    chunks = width // (3 * w)
    return pl.pallas_call(
        lambda *refs: pick_kernel(w, per, chunks, *refs),
        out_shape=(
            jax.ShapeDtypeStruct((per, 7 * w), BF16),
            jax.ShapeDtypeStruct((per, 2 * (width - 3 * w)), BF16),
        ),
        in_specs=[pl.BlockSpec(memory_space=pltpu.SMEM), pl.BlockSpec(memory_space=pl.ANY)],
        out_specs=(pl.BlockSpec(memory_space=pltpu.VMEM), pl.BlockSpec(memory_space=pltpu.VMEM)),
        scratch_shapes=[pltpu.VMEM((rows, width), BF16), pltpu.SemaphoreType.DMA((chunks,))],
        cost_estimate=pl.CostEstimate(
            flops=2 * 3 * per * rows * width, bytes_accessed=2 * rows * width, transcendentals=0
        ),
        name="pick",
    )(pivot_nodes, strip)


def boundary_kernel(w, near_ref, inverse_ref, boundary_ref, factor_ref, second_ref):
    near = near_ref[...]
    one_edge = near[:, w:2 * w]
    edge = near[:, 4 * w:]
    factor_at_two = rounded_dot(near[:, 2 * w:3 * w], inverse_ref[0])
    factor_at_edge = rounded_dot(edge[:, :w], inverse_ref[0])
    updated = reduced_by(edge[:, w:], factor_at_edge, near[:, :2 * w])
    second_edge = reduced_by(near[:, 3 * w:4 * w], factor_at_two, one_edge)
    factor_two = rounded_dot(updated[:, :w], inverse_ref[1])
    boundary_ref[...] = reduced_by(updated[:, w:], factor_two, second_edge)
    factor_ref[...] = factor_at_two
    second_ref[...] = second_edge


def boundary_of(near, inverses):
    w = near.shape[0]
    block = jax.ShapeDtypeStruct((w, w), BF16)
    vmem = pl.BlockSpec(memory_space=pltpu.VMEM)
    return pl.pallas_call(
        lambda *refs: boundary_kernel(w, *refs),
        out_shape=(block, block, block),
        in_specs=[vmem, vmem],
        out_specs=(vmem, vmem, vmem),
        cost_estimate=pl.CostEstimate(flops=14 * w * w * w, bytes_accessed=12 * w * 2 * w, transcendentals=0),
        name="boundary",
    )(near, inverses)


def trailing_kernel(
    w, panels_ref, block_ref, inverse_ref, near_ref, factor_ref, second_ref, far_one_ref, far_two_ref,
    out_ref, one_ref, two_ref,
):
    step = pl.program_id(0)

    def finish(one_rows, two_rows):
        updated = reduced_by(block_ref[...], one_ref[...], one_rows)
        out_ref[...] = reduced_by(updated, two_ref[...], two_rows)

    @pl.when(step == 0)
    def _():
        one_ref[...] = rounded_dot(panels_ref[:, :w], inverse_ref[0])
        panel = reduced_by(panels_ref[:, w:], one_ref[...], near_ref[:, :w])
        two_ref[...] = rounded_dot(panel, inverse_ref[1])
        finish(near_ref[:, w:], second_ref[...])

    @pl.when(step > 0)
    def _():
        one_rows = far_one_ref[...]
        finish(one_rows, reduced_by(far_two_ref[...], factor_ref[...], one_rows))


def trailing_of(strip, inverses, near, factor_at_two, second_edge, far):
    rows, width = strip.shape
    w = near.shape[0]
    steps = width // w - 2
    fixed = lambda i: (0, 0)
    return pl.pallas_call(
        lambda *refs: trailing_kernel(w, *refs),
        out_shape=jax.ShapeDtypeStruct((rows, width - 2 * w), BF16),
        grid=(steps,),
        in_specs=[
            pl.BlockSpec((rows, 2 * w), fixed),
            pl.BlockSpec((rows, w), lambda i: (0, i + 2)),
            pl.BlockSpec((2, w, w), lambda i: (0, 0, 0)),
            pl.BlockSpec((w, 2 * w), fixed),
            pl.BlockSpec((w, w), fixed),
            pl.BlockSpec((w, w), fixed),
            pl.BlockSpec((w, w), lambda i: (0, jnp.maximum(i - 1, 0))),
            pl.BlockSpec((w, w), lambda i: (0, steps - 1 + jnp.maximum(i - 1, 0))),
        ],
        out_specs=pl.BlockSpec((rows, w), lambda i: (0, i)),
        scratch_shapes=[pltpu.VMEM((rows, w), BF16), pltpu.VMEM((rows, w), BF16)],
        cost_estimate=pl.CostEstimate(
            flops=4 * rows * w * width, bytes_accessed=4 * rows * width + 4 * w * width, transcendentals=0
        ),
        name="trailing",
    )(strip, strip, inverses, near, factor_at_two, second_edge, far, far)


def body(panel_strip, pivot_inverses, coupling, pivot_nodes):
    strip = panel_strip[0]
    inverses = pivot_inverses[0]
    span = coupling[0]
    w = span.shape[0]
    blocks = lax.axis_size("blk")
    per = w // blocks

    back_one, back_two, back_three = (passed_along(span, "tm", by) for by in (1, 2, 3))

    near_here, far_here = picked_rows(pivot_nodes, strip, w, per)
    near = lax.all_gather(near_here, "blk", axis=0, tiled=True)
    boundary, factor_at_two, second_edge = boundary_of(near, inverses)
    back_one, back_two, back_three, boundary = lax.optimization_barrier(
        (back_one, back_two, back_three, boundary)
    )

    def advance(current, incoming, reach):
        return matmul_high(matmul_high(reach, incoming.astype(F32)), reach.T) + current

    incoming = passed_along(boundary, "tm", 1)
    span_two = matmul_high(span, back_one)
    span_four = matmul_high(span_two, matmul_high(back_two, back_three))
    incoming, span_four = lax.optimization_barrier((incoming, span_four))
    passed_four = passed_along(span_four, "tm", 4)
    span_four, far_here = lax.optimization_barrier((span_four, far_here))
    far = lax.all_to_all(jnp.tile(far_here, (blocks, 1)), "blk", 0, 0, tiled=True)
    current = advance(boundary.astype(F32), incoming, span)

    incoming = passed_along(current.astype(BF16), "tm", 2)
    current = advance(current, incoming, span_two)

    span_eight = matmul_high(span_four, passed_four)
    current, span_eight = lax.optimization_barrier((current, span_eight))
    incoming = passed_along(current.astype(BF16), "tm", 4)
    passed_eight = passed_along(span_eight, "tm", 8)
    current = advance(current, incoming, span_four)

    incoming = passed_along(current.astype(BF16), "tm", 8)
    span_sixteen = matmul_high(span_eight, passed_eight)
    incoming, span_sixteen = lax.optimization_barrier((incoming, span_sixteen))
    current = advance(current, incoming, span_eight)

    current, far = lax.optimization_barrier((current, far))
    incoming = passed_along(current.astype(BF16), "tm", 16)
    trailing = trailing_of(strip, inverses, near, factor_at_two, second_edge, far)
    incoming, trailing = lax.optimization_barrier((incoming, trailing))
    current = advance(current, incoming, span_sixteen)
    return (trailing[None], current[None])


def solution(mesh):
    placed = (P("tm", "blk", None), P("tm", None, None, None), P("tm", None, None), P())
    return jax.shard_map(
        body,
        mesh=mesh,
        in_specs=placed,
        out_specs=(P("tm", "blk", None), P("tm", None, None)),
        check_vma=False,
    )
```

```python
import jax
import jax.numpy as jnp
from jax import lax
from jax.experimental import pallas as pl
from jax.experimental.pallas import tpu as pltpu
from jax.sharding import PartitionSpec as P

BF16 = jnp.bfloat16
F32 = jnp.float32


def passed_along(x, axis, by):
    count = lax.axis_size(axis)
    return lax.ppermute(x, axis, [(i, i + by) for i in range(count - by)])


def matmul_high(left, right):
    return jnp.dot(left, right, precision=lax.Precision.HIGHEST, preferred_element_type=F32)


def rounded_dot(left, right):
    return jnp.dot(left, right, preferred_element_type=F32).astype(BF16)


def reduced_by(block, factor, rows):
    product = jnp.dot(factor, rows, preferred_element_type=F32)
    return (block.astype(F32) - product).astype(BF16)


def pick_kernel(w, per, chunks, nodes_hbm, strip_hbm, near_ref, far_ref, strip_ref, nodes_ref, sems):
    rows = strip_ref.shape[0]
    cols = strip_ref.shape[1] // chunks

    def part(i):
        at = pl.ds(i * cols, cols)
        return pltpu.make_async_copy(strip_hbm.at[:, at], strip_ref.at[:, at], sems.at[i])

    nodes = pltpu.make_async_copy(nodes_hbm, nodes_ref, sems.at[chunks])
    nodes.start()
    for i in range(chunks):
        part(i).start()
    nodes.wait()
    me = lax.axis_index("blk")
    lanes = 128
    at_row = lax.broadcasted_iota(jnp.int32, (3 * per, lanes), 0)
    at_lane = lax.broadcasted_iota(jnp.int32, (3 * per, lanes), 1)
    wanted = jnp.zeros((3 * per, lanes), jnp.int32)
    for k in range(3):
        for i in range(per):
            wanted = jnp.where(at_row == k * per + i, nodes_ref[k, me * per + i] - me * rows, wanted)
    picker = jnp.concatenate(
        [(wanted == at_lane + first).astype(F32).astype(BF16) for first in range(0, rows, lanes)], 1
    )
    far_width = strip_ref.shape[1] - 3 * w
    for i in range(chunks):
        part(i).wait()
        at = pl.ds(i * cols, cols)
        got = jnp.dot(picker, strip_ref[:, at], preferred_element_type=F32).astype(BF16)
        one, two, edge = got[:per], got[per:2 * per], got[2 * per:]
        if i == 0:
            near_ref[:, :2 * w] = one[:, w:]
            near_ref[:, 2 * w:3 * w] = two[:, :w]
            near_ref[:, 3 * w:4 * w] = two[:, 2 * w:]
            near_ref[:, 4 * w:] = edge
        else:
            for row in range(0, far_ref.shape[0], per):
                far_ref[row:row + per, (i - 1) * cols:i * cols] = one
                far_ref[row:row + per, far_width + (i - 1) * cols:far_width + i * cols] = two


def picked_rows(pivot_nodes, strip, w, per):
    rows, width = strip.shape
    chunks = width // (3 * w)
    return pl.pallas_call(
        lambda *refs: pick_kernel(w, per, chunks, *refs),
        out_shape=(pltpu.VMEM((per, 7 * w), BF16), pltpu.VMEM((w, 2 * (width - 3 * w)), BF16)),
        in_specs=[pl.BlockSpec(memory_space=pl.ANY), pl.BlockSpec(memory_space=pl.ANY)],
        out_specs=(pl.BlockSpec(memory_space=pltpu.VMEM), pl.BlockSpec(memory_space=pltpu.VMEM)),
        scratch_shapes=[
            pltpu.VMEM((rows, width), BF16),
            pltpu.SMEM(pivot_nodes.shape, jnp.int32),
            pltpu.SemaphoreType.DMA((chunks + 1,)),
        ],
        cost_estimate=pl.CostEstimate(
            flops=2 * 3 * per * rows * width, bytes_accessed=2 * rows * width, transcendentals=0
        ),
        name="pick",
    )(pivot_nodes, strip)


def boundary_kernel(w, near_ref, inverse_ref, boundary_ref, factor_ref, second_ref):
    near = near_ref[...]
    one_edge = near[:, w:2 * w]
    edge = near[:, 4 * w:]
    factor_at_two = rounded_dot(near[:, 2 * w:3 * w], inverse_ref[0])
    factor_at_edge = rounded_dot(edge[:, :w], inverse_ref[0])
    updated = reduced_by(edge[:, w:], factor_at_edge, near[:, :2 * w])
    second_edge = reduced_by(near[:, 3 * w:4 * w], factor_at_two, one_edge)
    factor_two = rounded_dot(updated[:, :w], inverse_ref[1])
    boundary_ref[...] = reduced_by(updated[:, w:], factor_two, second_edge)
    factor_ref[...] = factor_at_two
    second_ref[...] = second_edge


def boundary_of(near, inverses):
    w = near.shape[0]
    block = pltpu.VMEM((w, w), BF16)
    near = pltpu.with_memory_space_constraint(near, pltpu.VMEM)
    vmem = pl.BlockSpec(memory_space=pltpu.VMEM)
    return pl.pallas_call(
        lambda *refs: boundary_kernel(w, *refs),
        out_shape=(block, block, block),
        in_specs=[vmem, vmem],
        out_specs=(vmem, vmem, vmem),
        cost_estimate=pl.CostEstimate(flops=14 * w * w * w, bytes_accessed=12 * w * 2 * w, transcendentals=0),
        name="boundary",
    )(near, inverses)


def trailing_kernel(
    w, panels_ref, block_ref, inverse_ref, near_ref, factor_ref, second_ref, far_ref, out_ref, one_ref, two_ref
):
    step = pl.program_id(0)
    half = far_ref.shape[1] // 2

    def finish(one_rows, two_rows):
        updated = reduced_by(block_ref[...], one_ref[...], one_rows)
        out_ref[...] = reduced_by(updated, two_ref[...], two_rows)

    @pl.when(step == 0)
    def _():
        one_ref[...] = rounded_dot(panels_ref[:, :w], inverse_ref[0])
        panel = reduced_by(panels_ref[:, w:], one_ref[...], near_ref[:, :w])
        two_ref[...] = rounded_dot(panel, inverse_ref[1])
        finish(near_ref[:, w:2 * w], second_ref[...])

    @pl.when(step > 0)
    def _():
        at = pl.multiple_of((step - 1) * w, w)
        one_rows = far_ref[:, pl.ds(at, w)]
        finish(one_rows, reduced_by(far_ref[:, pl.ds(half + at, w)], factor_ref[...], one_rows))


def in_vmem(*arrays):
    return tuple(pltpu.with_memory_space_constraint(x, pltpu.VMEM) for x in arrays)


def trailing_of(strip, inverses, near, factor_at_two, second_edge, far):
    rows, width = strip.shape
    w = near.shape[0]
    vmem = pl.BlockSpec(memory_space=pltpu.VMEM)
    return pl.pallas_call(
        lambda *refs: trailing_kernel(w, *refs),
        out_shape=jax.ShapeDtypeStruct((rows, width - 2 * w), BF16),
        grid=(width // w - 2,),
        in_specs=[
            pl.BlockSpec((rows, 2 * w), lambda i: (0, 0)),
            pl.BlockSpec((rows, w), lambda i: (0, i + 2)),
            pl.BlockSpec((2, w, w), lambda i: (0, 0, 0)),
            vmem, vmem, vmem, vmem,
        ],
        out_specs=pl.BlockSpec((rows, w), lambda i: (0, i)),
        scratch_shapes=[pltpu.VMEM((rows, w), BF16), pltpu.VMEM((rows, w), BF16)],
        cost_estimate=pl.CostEstimate(
            flops=4 * rows * w * width, bytes_accessed=4 * rows * width + 4 * w * width, transcendentals=0
        ),
        name="trailing",
    )(strip, strip, inverses, *in_vmem(near, factor_at_two, second_edge, far))


def body(panel_strip, pivot_inverses, coupling, pivot_nodes):
    strip = panel_strip[0]
    inverses = pivot_inverses[0]
    span = coupling[0]
    w = span.shape[0]
    blocks = lax.axis_size("blk")
    per = w // blocks

    back_one, back_two, back_three = (passed_along(span, "tm", by) for by in (1, 2, 3))

    near_here, far_here = picked_rows(pivot_nodes, strip, w, per)
    near = lax.all_gather(near_here, "blk", axis=0, tiled=True)
    near, far_here = lax.optimization_barrier((near, far_here))
    far = lax.all_to_all(far_here, "blk", 0, 0, tiled=True)
    boundary, factor_at_two, second_edge = boundary_of(near, inverses)
    back_one, back_two, back_three, boundary = lax.optimization_barrier(
        (back_one, back_two, back_three, boundary)
    )

    def advance(current, incoming, reach):
        return matmul_high(matmul_high(reach, incoming.astype(F32)), reach.T) + current

    def half_product(reach, by):
        half = lax.dynamic_slice_in_dim(reach, lax.axis_index("blk") % 2 * (w // 2), w // 2, 1)
        return matmul_high(reach, passed_along(half, "tm", by))

    def joined(half):
        pairs = [[i, i + 1] for i in range(0, blocks, 2)]
        return lax.all_gather(half, "blk", axis=1, tiled=True, axis_index_groups=pairs)

    incoming = passed_along(boundary, "tm", 1)
    span_two = matmul_high(span, back_one)
    span_four = matmul_high(span_two, matmul_high(back_two, back_three))
    half_eight = half_product(span_four, 4)
    current = advance(boundary.astype(F32), incoming, span)

    incoming = passed_along(current.astype(BF16), "tm", 2)
    incoming, half_eight = lax.optimization_barrier((incoming, half_eight))
    current = advance(current, incoming, span_two)

    incoming = passed_along(current.astype(BF16), "tm", 4)
    span_eight = joined(half_eight)
    half_sixteen = half_product(span_eight, 8)
    incoming, span_eight = lax.optimization_barrier((incoming, span_eight))
    current = advance(current, incoming, span_four)

    incoming = passed_along(current.astype(BF16), "tm", 8)
    incoming, half_sixteen = lax.optimization_barrier((incoming, half_sixteen))
    current = advance(current, incoming, span_eight)

    current, far = lax.optimization_barrier((current, far))
    incoming = passed_along(current.astype(BF16), "tm", 16)
    span_sixteen = joined(half_sixteen)
    trailing = trailing_of(strip, inverses, near, factor_at_two, second_edge, far)
    incoming, trailing = lax.optimization_barrier((incoming, trailing))
    current = advance(current, incoming, span_sixteen)
    return (trailing[None], current[None])


def solution(mesh):
    placed = (P("tm", "blk", None), P("tm", None, None, None), P("tm", None, None), P())
    return jax.shard_map(
        body,
        mesh=mesh,
        in_specs=placed,
        out_specs=(P("tm", "blk", None), P("tm", None, None)),
        check_vma=False,
    )
```

```python
import jax
import jax.numpy as jnp
from jax import lax
from jax.experimental import pallas as pl
from jax.experimental.pallas import tpu as pltpu
from jax.sharding import PartitionSpec as P

BF16 = jnp.bfloat16
F32 = jnp.float32


def passed_along(x, axis, by):
    count = lax.axis_size(axis)
    return lax.ppermute(x, axis, [(i, i + by) for i in range(count - by)])


def matmul_high(left, right):
    return jnp.dot(left, right, precision=lax.Precision.HIGHEST, preferred_element_type=F32)


def rounded_dot(left, right):
    return jnp.dot(left, right, preferred_element_type=F32).astype(BF16)


def reduced_by(block, factor, rows):
    product = jnp.dot(factor, rows, preferred_element_type=F32)
    return (block.astype(F32) - product).astype(BF16)


def pick_kernel(w, per, chunks, nodes_hbm, strip_hbm, near_ref, far_ref, strip_ref, nodes_ref, sems):
    rows = strip_ref.shape[0]
    cols = strip_ref.shape[1] // chunks

    def part(i):
        at = pl.ds(i * cols, cols)
        return pltpu.make_async_copy(strip_hbm.at[:, at], strip_ref.at[:, at], sems.at[i])

    nodes = pltpu.make_async_copy(nodes_hbm, nodes_ref, sems.at[chunks])
    nodes.start()
    for i in range(chunks):
        part(i).start()
    nodes.wait()
    me = lax.axis_index("blk")
    lanes = 128
    at_row = lax.broadcasted_iota(jnp.int32, (3 * per, lanes), 0)
    at_lane = lax.broadcasted_iota(jnp.int32, (3 * per, lanes), 1)
    wanted = jnp.zeros((3 * per, lanes), jnp.int32)
    for k in range(3):
        for i in range(per):
            wanted = jnp.where(at_row == k * per + i, nodes_ref[k, me * per + i] - me * rows, wanted)
    picker = jnp.concatenate(
        [(wanted == at_lane + first).astype(F32).astype(BF16) for first in range(0, rows, lanes)], 1
    )
    far_width = strip_ref.shape[1] - 3 * w
    for i in range(chunks):
        part(i).wait()
        at = pl.ds(i * cols, cols)
        got = jnp.dot(picker, strip_ref[:, at], preferred_element_type=F32).astype(BF16)
        one, two, edge = got[:per], got[per:2 * per], got[2 * per:]
        if i == 0:
            near_ref[:, :2 * w] = one[:, w:]
            near_ref[:, 2 * w:3 * w] = two[:, :w]
            near_ref[:, 3 * w:4 * w] = two[:, 2 * w:]
            near_ref[:, 4 * w:] = edge
        else:
            for row in range(0, far_ref.shape[0], per):
                far_ref[row:row + per, (i - 1) * cols:i * cols] = one
                far_ref[row:row + per, far_width + (i - 1) * cols:far_width + i * cols] = two


def picked_rows(pivot_nodes, strip, w, per):
    rows, width = strip.shape
    chunks = width // (3 * w)
    return pl.pallas_call(
        lambda *refs: pick_kernel(w, per, chunks, *refs),
        out_shape=(
            pltpu.VMEM((per, 7 * w), BF16),
            pltpu.VMEM((w, 2 * (width - 3 * w)), BF16),
        ),
        in_specs=[pl.BlockSpec(memory_space=pl.ANY), pl.BlockSpec(memory_space=pl.ANY)],
        out_specs=tuple(pl.BlockSpec(memory_space=pltpu.VMEM) for _ in range(2)),
        scratch_shapes=[
            pltpu.VMEM((rows, width), BF16),
            pltpu.SMEM(pivot_nodes.shape, jnp.int32),
            pltpu.SemaphoreType.DMA((chunks + 1,)),
        ],
        cost_estimate=pl.CostEstimate(
            flops=2 * 3 * per * rows * width, bytes_accessed=2 * rows * width, transcendentals=0
        ),
        name="pick",
    )(pivot_nodes, strip)


def boundary_kernel(w, near_ref, inverse_ref, boundary_ref, factor_ref, second_ref):
    near = near_ref[...]
    one_edge = near[:, w:2 * w]
    edge = near[:, 4 * w:]
    factor_at_two = rounded_dot(near[:, 2 * w:3 * w], inverse_ref[0])
    factor_at_edge = rounded_dot(edge[:, :w], inverse_ref[0])
    updated = reduced_by(edge[:, w:], factor_at_edge, near[:, :2 * w])
    second_edge = reduced_by(near[:, 3 * w:4 * w], factor_at_two, one_edge)
    factor_two = rounded_dot(updated[:, :w], inverse_ref[1])
    boundary_ref[...] = reduced_by(updated[:, w:], factor_two, second_edge)
    factor_ref[...] = factor_at_two
    second_ref[...] = second_edge


def boundary_of(near, inverses):
    w = near.shape[0]
    block = pltpu.VMEM((w, w), BF16)
    near = pltpu.with_memory_space_constraint(near, pltpu.VMEM)
    vmem = pl.BlockSpec(memory_space=pltpu.VMEM)
    return pl.pallas_call(
        lambda *refs: boundary_kernel(w, *refs),
        out_shape=(block, block, block),
        in_specs=[vmem, vmem],
        out_specs=(vmem, vmem, vmem),
        cost_estimate=pl.CostEstimate(flops=14 * w * w * w, bytes_accessed=12 * w * 2 * w, transcendentals=0),
        name="boundary",
    )(near, inverses)


def trailing_kernel(
    w, strip_hbm, inverse_ref, near_ref, factor_ref, second_ref, far_ref, out_hbm, strip_ref, out_ref, sems
):
    half = far_ref.shape[1] // 2
    count = strip_ref.shape[1] // w

    def part(i):
        at = pl.ds(i * w, w)
        return pltpu.make_async_copy(strip_hbm.at[:, at], strip_ref.at[:, at], sems.at[0, i])

    def done_part(i):
        at = pl.ds(i * w, w)
        return pltpu.make_async_copy(out_ref.at[:, at], out_hbm.at[:, at], sems.at[1, i])

    for i in range(count):
        part(i).start()
    part(0).wait()
    first_factor = rounded_dot(strip_ref[:, :w], inverse_ref[0])
    part(1).wait()
    panel = reduced_by(strip_ref[:, w:2 * w], first_factor, near_ref[:, :w])
    second_factor = rounded_dot(panel, inverse_ref[1])
    for i in range(count - 2):
        if i == 0:
            one_rows, two_rows = near_ref[:, w:2 * w], second_ref[...]
        else:
            one_rows = far_ref[:, (i - 1) * w:i * w]
            two_rows = reduced_by(far_ref[:, half + (i - 1) * w:half + i * w], factor_ref[...], one_rows)
        part(i + 2).wait()
        updated = reduced_by(strip_ref[:, (i + 2) * w:(i + 3) * w], first_factor, one_rows)
        out_ref[:, i * w:(i + 1) * w] = reduced_by(updated, second_factor, two_rows)
        done_part(i).start()
    for i in range(count - 2):
        done_part(i).wait()


def in_vmem(*arrays):
    return tuple(pltpu.with_memory_space_constraint(x, pltpu.VMEM) for x in arrays)


def trailing_of(strip, inverses, near, factor_at_two, second_edge, far):
    rows, width = strip.shape
    w = near.shape[0]
    vmem = pl.BlockSpec(memory_space=pltpu.VMEM)
    return pl.pallas_call(
        lambda *refs: trailing_kernel(w, *refs),
        out_shape=jax.ShapeDtypeStruct((rows, width - 2 * w), BF16),
        in_specs=[pl.BlockSpec(memory_space=pl.ANY)] + [vmem] * 5,
        out_specs=pl.BlockSpec(memory_space=pl.ANY),
        scratch_shapes=[
            pltpu.VMEM((rows, width), BF16),
            pltpu.VMEM((rows, width - 2 * w), BF16),
            pltpu.SemaphoreType.DMA((2, width // w)),
        ],
        cost_estimate=pl.CostEstimate(
            flops=4 * rows * w * width, bytes_accessed=4 * rows * width + 4 * w * width, transcendentals=0
        ),
        name="trailing",
    )(strip, inverses, *in_vmem(near, factor_at_two, second_edge, far))


def body(panel_strip, pivot_inverses, coupling, pivot_nodes):
    strip = panel_strip[0]
    inverses = pivot_inverses[0]
    span = coupling[0]
    w = span.shape[0]
    blocks = lax.axis_size("blk")
    per = w // blocks

    back_one, back_two, back_three = (passed_along(span, "tm", by) for by in (1, 2, 3))

    near_here, far_here = picked_rows(pivot_nodes, strip, w, per)
    near = lax.all_gather(near_here, "blk", axis=0, tiled=True)
    near, far_here = lax.optimization_barrier((near, far_here))
    far = lax.all_to_all(far_here, "blk", 0, 0, tiled=True)
    boundary, factor_at_two, second_edge = boundary_of(near, inverses)
    back_one, back_two, back_three, boundary = lax.optimization_barrier(
        (back_one, back_two, back_three, boundary)
    )

    def advance(current, incoming, reach):
        return matmul_high(matmul_high(reach, incoming.astype(F32)), reach.T) + current

    def joined(half):
        pairs = [[i, i + 1] for i in range(0, blocks, 2)]
        return lax.all_gather(half, "blk", axis=1, tiled=True, axis_index_groups=pairs)

    arriving = [passed_along(boundary, "tm", by) for by in (1, 2, 3)]
    span_two = matmul_high(span, back_one)
    span_three = matmul_high(span_two, back_two)
    span_four = matmul_high(span_three, back_three)
    half_four = lax.dynamic_slice_in_dim(span_four, lax.axis_index("blk") % 2 * (w // 2), w // 2, 1)
    half_eight = matmul_high(span_four, passed_along(half_four, "tm", 4))
    current = boundary.astype(F32)
    for incoming, reach in zip(arriving, (span, span_two, span_three)):
        current = advance(current, incoming, reach)
    wire = current.astype(BF16)

    wire, half_eight = lax.optimization_barrier((wire, half_eight))
    incoming = passed_along(wire, "tm", 4)
    passed_eight = passed_along(half_eight, "tm", 8)
    span_eight = joined(half_eight)
    incoming, span_eight = lax.optimization_barrier((incoming, span_eight))
    current = advance(current, incoming, span_four)
    wire = current.astype(BF16)

    incoming = passed_along(wire, "tm", 8)
    half_sixteen = matmul_high(span_eight, passed_eight)
    span_sixteen = joined(half_sixteen)
    incoming, span_sixteen = lax.optimization_barrier((incoming, span_sixteen))
    current = advance(current, incoming, span_eight)
    wire = current.astype(BF16)

    wire, factor_at_two = lax.optimization_barrier((wire, factor_at_two))
    incoming = passed_along(wire, "tm", 16)
    trailing = trailing_of(strip, inverses, near, factor_at_two, second_edge, far)
    incoming, trailing = lax.optimization_barrier((incoming, trailing))
    current = advance(current, incoming, span_sixteen)
    return (trailing[None], current[None])


def solution(mesh):
    placed = (P("tm", "blk", None), P("tm", None, None, None), P("tm", None, None), P())
    return jax.shard_map(
        body,
        mesh=mesh,
        in_specs=placed,
        out_specs=(P("tm", "blk", None), P("tm", None, None)),
        check_vma=False,
    )
```

```python
import jax
import jax.numpy as jnp
from jax import lax
from jax.experimental import pallas as pl
from jax.experimental.pallas import tpu as pltpu
from jax.sharding import PartitionSpec as P

BF16 = jnp.bfloat16
F32 = jnp.float32
VMEM_BYTES = 16 << 20


def passed_along(x, axis, by):
    count = lax.axis_size(axis)
    return lax.ppermute(x, axis, [(i, i + by) for i in range(count - by)])


def matmul_high(left, right):
    return jnp.dot(left, right, precision=lax.Precision.HIGHEST, preferred_element_type=F32)


def rounded_dot(left, right):
    return jnp.dot(left, right, preferred_element_type=F32).astype(BF16)


def reduced_by(block, factor, rows):
    product = jnp.dot(factor, rows, preferred_element_type=F32)
    return (block.astype(F32) - product).astype(BF16)


def pick_kernel(w, per, chunks, nodes_hbm, strip_hbm, near_ref, far_ref, strip_ref, nodes_ref, sems):
    rows = strip_ref.shape[0]
    cols = strip_ref.shape[1] // chunks

    def part(i):
        at = pl.ds(i * cols, cols)
        return pltpu.make_async_copy(strip_hbm.at[:, at], strip_ref.at[:, at], sems.at[i])

    nodes = pltpu.make_async_copy(nodes_hbm, nodes_ref, sems.at[chunks])
    nodes.start()
    for i in range(chunks):
        part(i).start()
    nodes.wait()
    me = lax.axis_index("blk")
    lanes = 128
    at_row = lax.broadcasted_iota(jnp.int32, (3 * per, lanes), 0)
    at_lane = lax.broadcasted_iota(jnp.int32, (3 * per, lanes), 1)
    wanted = jnp.zeros((3 * per, lanes), jnp.int32)
    for k in range(3):
        for i in range(per):
            wanted = jnp.where(at_row == k * per + i, nodes_ref[k, me * per + i] - me * rows, wanted)
    picker = jnp.concatenate(
        [(wanted == at_lane + first).astype(F32).astype(BF16) for first in range(0, rows, lanes)], 1
    )
    width = far_ref.shape[1] // 2
    for i in range(chunks):
        part(i).wait()
        at = pl.ds(i * cols, cols)
        got = jnp.dot(picker, strip_ref[:, at], preferred_element_type=F32).astype(BF16)
        one, two, edge = got[:per], got[per:2 * per], got[2 * per:]
        if i == 0:
            near_ref[:, :2 * w] = one[:, w:]
            near_ref[:, 2 * w:3 * w] = two[:, :w]
            near_ref[:, 3 * w:4 * w] = two[:, 2 * w:]
            near_ref[:, 4 * w:] = edge
        else:
            for row in range((i - 1) * per, far_ref.shape[0], 2 * per):
                far_ref[row:row + per, :width] = one
                far_ref[row:row + per, width:] = two


def picked_rows(pivot_nodes, strip, w, per):
    rows, width = strip.shape
    chunks = width // (3 * w)
    return pl.pallas_call(
        lambda *refs: pick_kernel(w, per, chunks, *refs),
        out_shape=(
            pltpu.VMEM((per, 7 * w), BF16),
            pltpu.VMEM((w, width - 3 * w), BF16),
        ),
        in_specs=[pl.BlockSpec(memory_space=pltpu.HBM), pl.BlockSpec(memory_space=pltpu.HBM)],
        out_specs=tuple(pl.BlockSpec(memory_space=pltpu.VMEM) for _ in range(2)),
        scratch_shapes=[
            pltpu.VMEM((rows, width), BF16),
            pltpu.SMEM(pivot_nodes.shape, jnp.int32),
            pltpu.SemaphoreType.DMA((chunks + 1,)),
        ],
        cost_estimate=pl.CostEstimate(
            flops=2 * 3 * per * rows * width, bytes_accessed=2 * rows * width, transcendentals=0
        ),
        name="pick",
    )(pivot_nodes, strip)


def boundary_kernel(w, near_ref, inverse_ref, boundary_ref, factor_ref, second_ref, ones_ref):
    near = near_ref[...]
    one_edge = near[:, w:2 * w]
    edge = near[:, 4 * w:]
    factor_at_two = rounded_dot(near[:, 2 * w:3 * w], inverse_ref[0])
    factor_at_edge = rounded_dot(edge[:, :w], inverse_ref[0])
    updated = reduced_by(edge[:, w:], factor_at_edge, near[:, :2 * w])
    second_edge = reduced_by(near[:, 3 * w:4 * w], factor_at_two, one_edge)
    factor_two = rounded_dot(updated[:, :w], inverse_ref[1])
    boundary_ref[...] = reduced_by(updated[:, w:], factor_two, second_edge)
    factor_ref[...] = factor_at_two
    second_ref[...] = second_edge
    ones_ref[...] = near[:, :2 * w]


def boundary_of(near, inverses):
    w = near.shape[0]
    block = pltpu.VMEM((w, w), BF16)
    near = pltpu.with_memory_space_constraint(near, pltpu.VMEM)
    vmem = pl.BlockSpec(memory_space=pltpu.VMEM)
    return pl.pallas_call(
        lambda *refs: boundary_kernel(w, *refs),
        out_shape=(block, block, block, pltpu.VMEM((w, 2 * w), BF16)),
        in_specs=[vmem, vmem],
        out_specs=(vmem, vmem, vmem, vmem),
        cost_estimate=pl.CostEstimate(flops=14 * w * w * w, bytes_accessed=12 * w * 2 * w, transcendentals=0),
        compiler_params=pltpu.CompilerParams(vmem_limit_bytes=VMEM_BYTES),
        name="boundary",
    )(near, inverses)


def trailing_kernel(
    w, strip_hbm, inverse_ref, ones_ref, factor_ref, second_ref, own_ref, other_ref, out_hbm, strip_ref, out_ref, sems
):
    half = own_ref.shape[1] // 2
    per_half = half // w
    count = strip_ref.shape[1] // w
    core = lax.rem(lax.axis_index("blk"), 2)

    blocks = [0, 1, 2]
    for which in (core, 1 - core):
        blocks += [3 + which * per_half + k for k in range(per_half)]

    def columns(block):
        return pl.ds(block * w if isinstance(block, int) else pl.multiple_of(block * w, w), w)

    def part(i):
        at = columns(blocks[i])
        return pltpu.make_async_copy(strip_hbm.at[:, at], strip_ref.at[:, i * w:(i + 1) * w], sems.at[0, i])

    def done_part(i):
        at = columns(blocks[i] - 2)
        return pltpu.make_async_copy(out_ref.at[:, (i - 2) * w:(i - 1) * w], out_hbm.at[:, at], sems.at[1, i])

    for i in range(count):
        part(i).start()
    part(0).wait()
    first_factor = rounded_dot(strip_ref[:, :w], inverse_ref[0])
    part(1).wait()
    panel = reduced_by(strip_ref[:, w:2 * w], first_factor, ones_ref[:, :w])
    second_factor = rounded_dot(panel, inverse_ref[1])
    for i in range(2, count):
        if i == 2:
            one_rows, two_rows = ones_ref[:, w:2 * w], second_ref[...]
        else:
            ref, k = (own_ref, i - 3) if i - 3 < per_half else (other_ref, i - 3 - per_half)
            one_rows = ref[:, k * w:(k + 1) * w]
            two_rows = reduced_by(ref[:, half + k * w:half + (k + 1) * w], factor_ref[...], one_rows)
        part(i).wait()
        updated = reduced_by(strip_ref[:, i * w:(i + 1) * w], first_factor, one_rows)
        out_ref[:, (i - 2) * w:(i - 1) * w] = reduced_by(updated, second_factor, two_rows)
        done_part(i).start()
    for i in range(2, count):
        done_part(i).wait()


def in_vmem(*arrays):
    return tuple(pltpu.with_memory_space_constraint(x, pltpu.VMEM) for x in arrays)


def trailing_of(strip, inverses, ones, factor_at_two, second_edge, own, other):
    rows, width = strip.shape
    w = ones.shape[0]
    vmem = pl.BlockSpec(memory_space=pltpu.VMEM)
    return pl.pallas_call(
        lambda *refs: trailing_kernel(w, *refs),
        out_shape=jax.ShapeDtypeStruct((rows, width - 2 * w), BF16),
        in_specs=[pl.BlockSpec(memory_space=pltpu.HBM)] + [vmem] * 6,
        out_specs=pl.BlockSpec(memory_space=pl.ANY),
        scratch_shapes=[
            pltpu.VMEM((rows, width), BF16),
            pltpu.VMEM((rows, width - 2 * w), BF16),
            pltpu.SemaphoreType.DMA((2, width // w)),
        ],
        cost_estimate=pl.CostEstimate(
            flops=4 * rows * w * width, bytes_accessed=4 * rows * width + 4 * w * width, transcendentals=0
        ),
        name="trailing",
    )(strip, inverses, *in_vmem(ones, factor_at_two, second_edge, own, other))


def body(panel_strip, pivot_inverses, coupling, pivot_nodes):
    strip = panel_strip[0]
    inverses = pivot_inverses[0]
    span = coupling[0]
    w = span.shape[0]
    blocks = lax.axis_size("blk")
    per = w // blocks

    back_one, back_two, back_three = (passed_along(span, "tm", by) for by in (1, 2, 3))

    near_here, far_here = picked_rows(pivot_nodes, strip, w, per)
    near = lax.all_gather(near_here, "blk", axis=0, tiled=True)
    boundary, factor_at_two, second_edge, one_rows = boundary_of(near, inverses)
    back_one, back_two, back_three, boundary = lax.optimization_barrier(
        (back_one, back_two, back_three, boundary)
    )

    def advance(current, incoming, reach):
        return matmul_high(matmul_high(reach, incoming.astype(F32)), reach.T) + current

    def joined(half):
        pairs = [[i, i + 1] for i in range(0, blocks, 2)]
        return lax.all_gather(half, "blk", axis=1, tiled=True, axis_index_groups=pairs)

    arriving = [passed_along(boundary, "tm", by) for by in (1, 2, 3)]
    arriving[0], far_here = lax.optimization_barrier((arriving[0], far_here))
    own = lax.all_to_all(far_here, "blk", 0, 0, tiled=True)
    span_two = matmul_high(span, back_one)
    span_three = matmul_high(span_two, back_two)
    span_four = matmul_high(span_three, back_three)
    half_four = lax.dynamic_slice_in_dim(span_four, lax.axis_index("blk") % 2 * (w // 2), w // 2, 1)
    half_eight = matmul_high(span_four, passed_along(half_four, "tm", 4))
    current = boundary.astype(F32)
    for incoming, reach in zip(arriving, (span, span_two, span_three)):
        current = advance(current, incoming, reach)
    wire = current.astype(BF16)

    incoming = passed_along(wire, "tm", 4)
    passed_eight = passed_along(half_eight, "tm", 8)
    span_eight = joined(half_eight)
    incoming, span_eight = lax.optimization_barrier((incoming, span_eight))
    current = advance(current, incoming, span_four)
    wire = current.astype(BF16)

    incoming = passed_along(wire, "tm", 8)
    other = lax.ppermute(own, "blk", [(i, i ^ 1) for i in range(blocks)])
    span_sixteen = joined(matmul_high(span_eight, passed_eight))
    current = advance(current, incoming, span_eight)
    wire = current.astype(BF16)

    wire, factor_at_two = lax.optimization_barrier((wire, factor_at_two))
    incoming = passed_along(wire, "tm", 16)
    trailing = trailing_of(strip, inverses, one_rows, factor_at_two, second_edge, own, other)
    incoming, trailing = lax.optimization_barrier((incoming, trailing))
    current = advance(current, incoming, span_sixteen)
    return (trailing[None], current[None])


def solution(mesh):
    placed = (P("tm", "blk", None), P("tm", None, None, None), P("tm", None, None), P())
    return jax.shard_map(
        body,
        mesh=mesh,
        in_specs=placed,
        out_specs=(P("tm", "blk", None), P("tm", None, None)),
        check_vma=False,
    )
```

```python
import jax
import jax.numpy as jnp
from jax import lax
from jax.experimental import pallas as pl
from jax.experimental.pallas import tpu as pltpu
from jax.sharding import PartitionSpec as P

BF16 = jnp.bfloat16
F32 = jnp.float32
VMEM_BYTES = 16 << 20


def passed_along(x, axis, by):
    count = lax.axis_size(axis)
    return lax.ppermute(x, axis, [(i, i + by) for i in range(count - by)])


def matmul_high(left, right):
    return jnp.dot(left, right, precision=lax.Precision.HIGHEST, preferred_element_type=F32)


def rounded_dot(left, right):
    return jnp.dot(left, right, preferred_element_type=F32).astype(BF16)


def reduced_by(block, factor, rows):
    product = jnp.dot(factor, rows, preferred_element_type=F32)
    return (block.astype(F32) - product).astype(BF16)


def pick_kernel(w, per, chunks, nodes_hbm, strip_hbm, near_ref, far_ref, strip_ref, nodes_ref, sems):
    rows = strip_ref.shape[0]
    cols = strip_ref.shape[1] // chunks

    def part(i):
        at = pl.ds(i * cols, cols)
        return pltpu.make_async_copy(strip_hbm.at[:, at], strip_ref.at[:, at], sems.at[i])

    nodes = pltpu.make_async_copy(nodes_hbm, nodes_ref, sems.at[chunks])
    nodes.start()
    for i in range(chunks):
        part(i).start()
    nodes.wait()
    me = lax.axis_index("blk")
    lanes = 128
    at_row = lax.broadcasted_iota(jnp.int32, (3 * per, lanes), 0)
    at_lane = lax.broadcasted_iota(jnp.int32, (3 * per, lanes), 1)
    wanted = jnp.zeros((3 * per, lanes), jnp.int32)
    for k in range(3):
        for i in range(per):
            wanted = jnp.where(at_row == k * per + i, nodes_ref[k, me * per + i] - me * rows, wanted)
    picker = jnp.concatenate(
        [(wanted == at_lane + first).astype(F32).astype(BF16) for first in range(0, rows, lanes)], 1
    )
    width = far_ref.shape[1] // 2
    for i in range(chunks):
        part(i).wait()
        at = pl.ds(i * cols, cols)
        got = jnp.dot(picker, strip_ref[:, at], preferred_element_type=F32).astype(BF16)
        one, two, edge = got[:per], got[per:2 * per], got[2 * per:]
        if i == 0:
            near_ref[:, :2 * w] = one[:, w:]
            near_ref[:, 2 * w:3 * w] = two[:, :w]
            near_ref[:, 3 * w:4 * w] = two[:, 2 * w:]
            near_ref[:, 4 * w:] = edge
        else:
            for row in range((i - 1) * per, far_ref.shape[0], 2 * per):
                far_ref[row:row + per, :width] = one
                far_ref[row:row + per, width:] = two


def picked_rows(pivot_nodes, strip, w, per):
    rows, width = strip.shape
    chunks = width // (3 * w)
    return pl.pallas_call(
        lambda *refs: pick_kernel(w, per, chunks, *refs),
        out_shape=(
            pltpu.VMEM((per, 7 * w), BF16),
            pltpu.VMEM((w, width - 3 * w), BF16),
        ),
        in_specs=[pl.BlockSpec(memory_space=pltpu.HBM), pl.BlockSpec(memory_space=pltpu.HBM)],
        out_specs=tuple(pl.BlockSpec(memory_space=pltpu.VMEM) for _ in range(2)),
        scratch_shapes=[
            pltpu.VMEM((rows, width), BF16),
            pltpu.SMEM(pivot_nodes.shape, jnp.int32),
            pltpu.SemaphoreType.DMA((chunks + 1,)),
        ],
        cost_estimate=pl.CostEstimate(
            flops=2 * 3 * per * rows * width, bytes_accessed=2 * rows * width, transcendentals=0
        ),
        name="pick",
    )(pivot_nodes, strip)


def boundary_kernel(w, near_ref, inverse_ref, boundary_ref, factor_ref, second_ref, ones_ref):
    near = near_ref[...]
    one_edge = near[:, w:2 * w]
    edge = near[:, 4 * w:]
    factor_at_two = rounded_dot(near[:, 2 * w:3 * w], inverse_ref[0])
    factor_at_edge = rounded_dot(edge[:, :w], inverse_ref[0])
    updated = reduced_by(edge[:, w:], factor_at_edge, near[:, :2 * w])
    second_edge = reduced_by(near[:, 3 * w:4 * w], factor_at_two, one_edge)
    factor_two = rounded_dot(updated[:, :w], inverse_ref[1])
    boundary_ref[...] = reduced_by(updated[:, w:], factor_two, second_edge)
    factor_ref[...] = factor_at_two
    second_ref[...] = second_edge
    ones_ref[...] = near[:, :2 * w]


def boundary_of(near, inverses):
    w = near.shape[0]
    block = pltpu.VMEM((w, w), BF16)
    near = pltpu.with_memory_space_constraint(near, pltpu.VMEM)
    vmem = pl.BlockSpec(memory_space=pltpu.VMEM)
    return pl.pallas_call(
        lambda *refs: boundary_kernel(w, *refs),
        out_shape=(block, block, block, pltpu.VMEM((w, 2 * w), BF16)),
        in_specs=[vmem, vmem],
        out_specs=(vmem, vmem, vmem, vmem),
        cost_estimate=pl.CostEstimate(flops=14 * w * w * w, bytes_accessed=12 * w * 2 * w, transcendentals=0),
        compiler_params=pltpu.CompilerParams(vmem_limit_bytes=VMEM_BYTES),
        name="boundary",
    )(near, inverses)


def edge_kernel(
    w, strip_hbm, inverse_ref, ones_ref, second_ref, out_hbm, one_ref, two_ref, strip_ref, edge_ref, sems
):
    def part(i):
        at = pl.ds(i * w, w)
        return pltpu.make_async_copy(strip_hbm.at[:, at], strip_ref.at[:, at], sems.at[i])

    for i in range(3):
        part(i).start()
    part(0).wait()
    one_ref[...] = rounded_dot(strip_ref[:, :w], inverse_ref[0])
    part(1).wait()
    panel = reduced_by(strip_ref[:, w:2 * w], one_ref[...], ones_ref[:, :w])
    two_ref[...] = rounded_dot(panel, inverse_ref[1])
    part(2).wait()
    updated = reduced_by(strip_ref[:, 2 * w:], one_ref[...], ones_ref[:, w:])
    edge_ref[...] = reduced_by(updated, two_ref[...], second_ref[...])
    done = pltpu.make_async_copy(edge_ref, out_hbm.at[:, pl.ds(0, w)], sems.at[3])
    done.start()
    done.wait()


def far_kernel(
    w, strip_hbm, begun_hbm, one_ref, two_ref, factor_ref, own_ref, other_ref, out_hbm, strip_ref, out_ref, sems
):
    del begun_hbm
    half = own_ref.shape[1] // 2
    per_half = half // w
    count = 2 * per_half
    core = lax.rem(lax.axis_index("blk"), 2)

    blocks = [which * per_half + k for which in (core, 1 - core) for k in range(per_half)]

    def columns(block):
        return pl.ds(pl.multiple_of(block * w, w), w)

    def part(i):
        at = columns(blocks[i] + 3)
        return pltpu.make_async_copy(strip_hbm.at[:, at], strip_ref.at[:, i * w:(i + 1) * w], sems.at[0, i])

    def done_part(i):
        at = columns(blocks[i] + 1)
        return pltpu.make_async_copy(out_ref.at[:, i * w:(i + 1) * w], out_hbm.at[:, at], sems.at[1, i])

    for i in range(count):
        part(i).start()
    for i in range(count):
        ref, k = (own_ref, i) if i < per_half else (other_ref, i - per_half)
        one_rows = ref[:, k * w:(k + 1) * w]
        two_rows = reduced_by(ref[:, half + k * w:half + (k + 1) * w], factor_ref[...], one_rows)
        part(i).wait()
        updated = reduced_by(strip_ref[:, i * w:(i + 1) * w], one_ref[...], one_rows)
        out_ref[:, i * w:(i + 1) * w] = reduced_by(updated, two_ref[...], two_rows)
        done_part(i).start()
    for i in range(count):
        done_part(i).wait()


def in_vmem(*arrays):
    return tuple(pltpu.with_memory_space_constraint(x, pltpu.VMEM) for x in arrays)


def trailing_edge(strip, inverses, ones, second_edge):
    rows, width = strip.shape
    w = ones.shape[0]
    vmem, hbm = pl.BlockSpec(memory_space=pltpu.VMEM), pl.BlockSpec(memory_space=pl.ANY)
    return pl.pallas_call(
        lambda *refs: edge_kernel(w, *refs),
        out_shape=(
            jax.ShapeDtypeStruct((rows, width - 2 * w), BF16),
            pltpu.VMEM((rows, w), BF16),
            pltpu.VMEM((rows, w), BF16),
        ),
        in_specs=[hbm, vmem, vmem, vmem],
        out_specs=(hbm, vmem, vmem),
        scratch_shapes=[
            pltpu.VMEM((rows, 3 * w), BF16),
            pltpu.VMEM((rows, w), BF16),
            pltpu.SemaphoreType.DMA((4,)),
        ],
        cost_estimate=pl.CostEstimate(
            flops=10 * rows * w * w, bytes_accessed=12 * rows * w, transcendentals=0
        ),
        name="edge",
    )(strip, inverses, *in_vmem(ones, second_edge))


def trailing_far(strip, begun, factors, factor_at_two, own, other):
    rows, width = strip.shape
    w = factor_at_two.shape[0]
    blocks = width // w - 3
    vmem, hbm = pl.BlockSpec(memory_space=pltpu.VMEM), pl.BlockSpec(memory_space=pl.ANY)
    return pl.pallas_call(
        lambda *refs: far_kernel(w, *refs),
        out_shape=jax.ShapeDtypeStruct(begun.shape, BF16),
        in_specs=[hbm, hbm] + [vmem] * 5,
        out_specs=hbm,
        input_output_aliases={1: 0},
        scratch_shapes=[
            pltpu.VMEM((rows, blocks * w), BF16),
            pltpu.VMEM((rows, blocks * w), BF16),
            pltpu.SemaphoreType.DMA((2, blocks)),
        ],
        cost_estimate=pl.CostEstimate(
            flops=w, bytes_accessed=w, transcendentals=0
        ),
        name="far",
    )(strip, begun, *in_vmem(*factors, factor_at_two, own, other))


def after(x, gate):
    return lax.optimization_barrier((x, gate))[0]


def body(panel_strip, pivot_inverses, coupling, pivot_nodes):
    strip = panel_strip[0]
    inverses = pivot_inverses[0]
    span = coupling[0]
    w = span.shape[0]
    blocks = lax.axis_size("blk")
    per = w // blocks

    back_one, back_two, back_three = (passed_along(span, "tm", by) for by in (1, 2, 3))

    near_here, far_here = picked_rows(pivot_nodes, strip, w, per)
    near = lax.all_gather(near_here, "blk", axis=0, tiled=True)
    near, far_here = lax.optimization_barrier((near, far_here))
    own = lax.all_to_all(far_here, "blk", 0, 0, tiled=True)
    boundary, factor_at_two, second_edge, one_rows = boundary_of(near, inverses)
    back_one, back_two, back_three, boundary = lax.optimization_barrier(
        (back_one, back_two, back_three, boundary)
    )

    def advance(current, incoming, reach):
        return matmul_high(matmul_high(reach, incoming.astype(F32)), reach.T) + current

    def joined(half):
        pairs = [[i, i + 1] for i in range(0, blocks, 2)]
        return lax.all_gather(half, "blk", axis=1, tiled=True, axis_index_groups=pairs)

    arriving = [passed_along(boundary, "tm", by) for by in (1, 2, 3)]
    span_two = matmul_high(span, back_one)
    span_three = matmul_high(span_two, back_two)
    span_four = matmul_high(span_three, back_three)
    half_four = lax.dynamic_slice_in_dim(span_four, lax.axis_index("blk") % 2 * (w // 2), w // 2, 1)
    half_eight = matmul_high(span_four, passed_along(half_four, "tm", 4))
    current = boundary.astype(F32)
    for incoming, reach in zip(arriving, (span, span_two, span_three)):
        current = advance(current, incoming, reach)
    wire = current.astype(BF16)

    incoming = passed_along(wire, "tm", 4)
    passed_eight = passed_along(half_eight, "tm", 8)
    span_eight = joined(half_eight)
    incoming, span_eight = lax.optimization_barrier((incoming, span_eight))
    current = advance(current, incoming, span_four)
    wire = current.astype(BF16)

    incoming = passed_along(wire, "tm", 8)
    other = lax.ppermute(after(own, wire), "blk", [(i, i ^ 1) for i in range(blocks)])
    begun, *factors = trailing_edge(strip, inverses, after(one_rows, wire), second_edge)
    half_sixteen = matmul_high(span_eight, passed_eight)
    incoming, begun, half_sixteen = lax.optimization_barrier((incoming, begun, half_sixteen))
    span_sixteen = joined(half_sixteen)
    current = advance(current, incoming, span_eight)
    wire = current.astype(BF16)

    incoming = passed_along(wire, "tm", 16)
    trailing = trailing_far(strip, begun, factors, factor_at_two, own, other)
    incoming, trailing = lax.optimization_barrier((incoming, trailing))
    current = advance(current, incoming, span_sixteen)
    return (trailing[None], current[None])


def solution(mesh):
    placed = (P("tm", "blk", None), P("tm", None, None, None), P("tm", None, None), P())
    return jax.shard_map(
        body,
        mesh=mesh,
        in_specs=placed,
        out_specs=(P("tm", "blk", None), P("tm", None, None)),
        check_vma=False,
    )
```

```python
import jax
import jax.numpy as jnp
from jax import lax
from jax.experimental import pallas as pl
from jax.experimental.pallas import tpu as pltpu
from jax.sharding import PartitionSpec as P

BF16 = jnp.bfloat16
F32 = jnp.float32
VMEM_BYTES = 16 << 20


def passed_along(x, axis, by):
    count = lax.axis_size(axis)
    return lax.ppermute(x, axis, [(i, i + by) for i in range(count - by)])


def matmul_high(left, right):
    return jnp.dot(left, right, precision=lax.Precision.HIGHEST, preferred_element_type=F32)


def rounded_dot(left, right):
    return jnp.dot(left, right, preferred_element_type=F32).astype(BF16)


def reduced_by(block, factor, rows):
    product = jnp.dot(factor, rows, preferred_element_type=F32)
    return (block.astype(F32) - product).astype(BF16)


def pick_kernel(w, per, chunks, nodes_hbm, strip_hbm, near_ref, far_hbm, strip_ref, nodes_ref, far_ref, sems, far_sems):
    rows = strip_ref.shape[0]
    cols = strip_ref.shape[1] // chunks

    def part(i):
        at = pl.ds(i * cols, cols)
        return pltpu.make_async_copy(strip_hbm.at[:, at], strip_ref.at[:, at], sems.at[i])

    nodes = pltpu.make_async_copy(nodes_hbm, nodes_ref, sems.at[chunks])
    nodes.start()
    for i in [*range(1, chunks), 0]:
        part(i).start()
    nodes.wait()
    me = lax.axis_index("blk")
    lanes = 128
    at_row = lax.broadcasted_iota(jnp.int32, (3 * per, lanes), 0)
    at_lane = lax.broadcasted_iota(jnp.int32, (3 * per, lanes), 1)
    wanted = jnp.zeros((3 * per, lanes), jnp.int32)
    for k in range(3):
        for i in range(per):
            wanted = jnp.where(at_row == k * per + i, nodes_ref[k, me * per + i] - me * rows, wanted)
    picker = jnp.concatenate(
        [(wanted == at_lane + first).astype(F32).astype(BF16) for first in range(0, rows, lanes)], 1
    )
    width = far_ref.shape[2] // 2
    copies = []
    for i in [*range(1, chunks), 0]:
        part(i).wait()
        at = pl.ds(i * cols, cols)
        got = jnp.dot(picker, strip_ref[:, at], preferred_element_type=F32).astype(BF16)
        one, two, edge = got[:per], got[per:2 * per], got[2 * per:]
        if i == 0:
            near_ref[:, :2 * w] = one[:, w:]
            near_ref[:, 2 * w:3 * w] = two[:, :w]
            near_ref[:, 3 * w:4 * w] = two[:, 2 * w:]
            near_ref[:, 4 * w:] = edge
        else:
            far_ref[i - 1, :, :width] = one
            far_ref[i - 1, :, width:] = two
            for row in range((i - 1) * per, far_hbm.shape[0], 2 * per):
                copies.append(
                    pltpu.make_async_copy(
                        far_ref.at[i - 1], far_hbm.at[pl.ds(row, per), :], far_sems.at[row // per]
                    )
                )
                copies[-1].start()
    for copy in copies:
        copy.wait()


def picked_rows(pivot_nodes, strip, w, per):
    rows, width = strip.shape
    chunks = width // (3 * w)
    return pl.pallas_call(
        lambda *refs: pick_kernel(w, per, chunks, *refs),
        out_shape=(
            pltpu.VMEM((per, 7 * w), BF16),
            jax.ShapeDtypeStruct((w, width - 3 * w), BF16),
        ),
        in_specs=[pl.BlockSpec(memory_space=pltpu.HBM), pl.BlockSpec(memory_space=pltpu.HBM)],
        out_specs=(pl.BlockSpec(memory_space=pltpu.VMEM), pl.BlockSpec(memory_space=pl.ANY)),
        scratch_shapes=[
            pltpu.VMEM((rows, width), BF16),
            pltpu.SMEM(pivot_nodes.shape, jnp.int32),
            pltpu.VMEM((chunks - 1, per, width - 3 * w), BF16),
            pltpu.SemaphoreType.DMA((chunks + 1,)),
            pltpu.SemaphoreType.DMA((w // per,)),
        ],
        cost_estimate=pl.CostEstimate(
            flops=2 * 3 * per * rows * width, bytes_accessed=2 * rows * width, transcendentals=0
        ),
        name="pick",
    )(pivot_nodes, strip)


def boundary_kernel(w, near_ref, inverse_ref, boundary_ref, factor_ref, second_ref, ones_ref):
    near = near_ref[...]
    one_edge = near[:, w:2 * w]
    edge = near[:, 4 * w:]
    factor_at_two = rounded_dot(near[:, 2 * w:3 * w], inverse_ref[0])
    factor_at_edge = rounded_dot(edge[:, :w], inverse_ref[0])
    updated = reduced_by(edge[:, w:], factor_at_edge, near[:, :2 * w])
    second_edge = reduced_by(near[:, 3 * w:4 * w], factor_at_two, one_edge)
    factor_two = rounded_dot(updated[:, :w], inverse_ref[1])
    boundary_ref[...] = reduced_by(updated[:, w:], factor_two, second_edge)
    factor_ref[...] = factor_at_two
    second_ref[...] = second_edge
    ones_ref[...] = near[:, :2 * w]


def boundary_of(near, inverses):
    w = near.shape[0]
    block = pltpu.VMEM((w, w), BF16)
    near = pltpu.with_memory_space_constraint(near, pltpu.VMEM)
    vmem = pl.BlockSpec(memory_space=pltpu.VMEM)
    return pl.pallas_call(
        lambda *refs: boundary_kernel(w, *refs),
        out_shape=(block, block, block, pltpu.VMEM((w, 2 * w), BF16)),
        in_specs=[vmem, vmem],
        out_specs=(vmem, vmem, vmem, vmem),
        cost_estimate=pl.CostEstimate(flops=14 * w * w * w, bytes_accessed=12 * w * 2 * w, transcendentals=0),
        compiler_params=pltpu.CompilerParams(vmem_limit_bytes=VMEM_BYTES),
        name="boundary",
    )(near, inverses)


def edge_kernel(
    w, strip_hbm, inverse_ref, ones_ref, second_ref, out_hbm, one_ref, two_ref, strip_ref, edge_ref, sems
):
    def part(i):
        at = pl.ds(i * w, w)
        return pltpu.make_async_copy(strip_hbm.at[:, at], strip_ref.at[:, at], sems.at[i])

    for i in range(3):
        part(i).start()
    part(0).wait()
    one_ref[...] = rounded_dot(strip_ref[:, :w], inverse_ref[0])
    part(1).wait()
    panel = reduced_by(strip_ref[:, w:2 * w], one_ref[...], ones_ref[:, :w])
    two_ref[...] = rounded_dot(panel, inverse_ref[1])
    part(2).wait()
    updated = reduced_by(strip_ref[:, 2 * w:], one_ref[...], ones_ref[:, w:])
    edge_ref[...] = reduced_by(updated, two_ref[...], second_ref[...])
    done = pltpu.make_async_copy(edge_ref, out_hbm.at[:, pl.ds(0, w)], sems.at[3])
    done.start()
    done.wait()


def far_kernel(
    w, strip_hbm, begun_hbm, own_hbm, other_ref, one_ref, two_ref, factor_ref, out_hbm,
    strip_ref, own_ref, out_ref, sems, own_sem,
):
    del begun_hbm
    half = own_hbm.shape[1] // 2
    per_half = half // w
    count = 2 * per_half
    core = lax.rem(lax.axis_index("blk"), 2)

    blocks = [which * per_half + k for which in (core, 1 - core) for k in range(per_half)]

    def columns(block):
        return pl.ds(pl.multiple_of(block * w, w), w)

    def part(i):
        at = columns(blocks[i] + 3)
        return pltpu.make_async_copy(strip_hbm.at[:, at], strip_ref.at[:, i * w:(i + 1) * w], sems.at[0, i])

    def done_part(i):
        at = columns(blocks[i] + 1)
        return pltpu.make_async_copy(out_ref.at[:, i * w:(i + 1) * w], out_hbm.at[:, at], sems.at[1, i])

    own = pltpu.make_async_copy(own_hbm, own_ref, own_sem)
    own.start()
    for i in range(count):
        part(i).start()
    own.wait()
    for i in range(count):
        ref, k = (own_ref, i) if i < per_half else (other_ref, i - per_half)
        one_rows = ref[:, k * w:(k + 1) * w]
        two_rows = reduced_by(ref[:, half + k * w:half + (k + 1) * w], factor_ref[...], one_rows)
        part(i).wait()
        updated = reduced_by(strip_ref[:, i * w:(i + 1) * w], one_ref[...], one_rows)
        out_ref[:, i * w:(i + 1) * w] = reduced_by(updated, two_ref[...], two_rows)
        done_part(i).start()
    for i in range(count):
        done_part(i).wait()


def in_vmem(*arrays):
    return tuple(pltpu.with_memory_space_constraint(x, pltpu.VMEM) for x in arrays)


def trailing_edge(strip, inverses, ones, second_edge):
    rows, width = strip.shape
    w = ones.shape[0]
    vmem, hbm = pl.BlockSpec(memory_space=pltpu.VMEM), pl.BlockSpec(memory_space=pl.ANY)
    return pl.pallas_call(
        lambda *refs: edge_kernel(w, *refs),
        out_shape=(
            jax.ShapeDtypeStruct((rows, width - 2 * w), BF16),
            pltpu.VMEM((rows, w), BF16),
            pltpu.VMEM((rows, w), BF16),
        ),
        in_specs=[hbm, vmem, vmem, vmem],
        out_specs=(hbm, vmem, vmem),
        scratch_shapes=[
            pltpu.VMEM((rows, 3 * w), BF16),
            pltpu.VMEM((rows, w), BF16),
            pltpu.SemaphoreType.DMA((4,)),
        ],
        cost_estimate=pl.CostEstimate(
            flops=w, bytes_accessed=w, transcendentals=0
        ),
        name="edge",
    )(strip, inverses, *in_vmem(ones, second_edge))


def trailing_far(strip, begun, factors, factor_at_two, own, other):
    rows, width = strip.shape
    w = factor_at_two.shape[0]
    blocks = width // w - 3
    vmem, hbm = pl.BlockSpec(memory_space=pltpu.VMEM), pl.BlockSpec(memory_space=pl.ANY)
    return pl.pallas_call(
        lambda *refs: far_kernel(w, *refs),
        out_shape=jax.ShapeDtypeStruct(begun.shape, BF16),
        in_specs=[hbm] * 3 + [vmem] * 4,
        out_specs=hbm,
        input_output_aliases={1: 0},
        scratch_shapes=[
            pltpu.VMEM((rows, blocks * w), BF16),
            pltpu.VMEM(own.shape, BF16),
            pltpu.VMEM((rows, blocks * w), BF16),
            pltpu.SemaphoreType.DMA((2, blocks)),
            pltpu.SemaphoreType.DMA,
        ],
        cost_estimate=pl.CostEstimate(
            flops=w, bytes_accessed=w, transcendentals=0
        ),
        name="far",
    )(strip, begun, own, *in_vmem(other, *factors, factor_at_two))


def after(x, gate):
    return lax.optimization_barrier((x, gate))[0]


def body(panel_strip, pivot_inverses, coupling, pivot_nodes):
    strip = panel_strip[0]
    inverses = pivot_inverses[0]
    span = coupling[0]
    w = span.shape[0]
    blocks = lax.axis_size("blk")
    per = w // blocks

    back_one, back_two, back_three = (passed_along(span, "tm", by) for by in (1, 2, 3))

    near_here, far_here = picked_rows(pivot_nodes, strip, w, per)
    near = lax.all_gather(near_here, "blk", axis=0, tiled=True)
    near, far_here = lax.optimization_barrier((near, far_here))
    own = lax.all_to_all(far_here, "blk", 0, 0, tiled=True)
    boundary, factor_at_two, second_edge, one_rows = boundary_of(near, inverses)
    back_one, back_two, back_three, boundary = lax.optimization_barrier(
        (back_one, back_two, back_three, boundary)
    )

    def advance(current, incoming, reach):
        return matmul_high(matmul_high(reach, incoming.astype(F32)), reach.T) + current

    def joined(half):
        pairs = [[i, i + 1] for i in range(0, blocks, 2)]
        return lax.all_gather(half, "blk", axis=1, tiled=True, axis_index_groups=pairs)

    arriving = [passed_along(boundary, "tm", by) for by in (1, 2, 3)]
    span_two = matmul_high(span, back_one)
    span_three = matmul_high(span_two, back_two)
    span_four = matmul_high(span_three, back_three)
    half_four = lax.dynamic_slice_in_dim(span_four, lax.axis_index("blk") % 2 * (w // 2), w // 2, 1)
    half_eight = matmul_high(span_four, passed_along(half_four, "tm", 4))
    current = boundary.astype(F32)
    for incoming, reach in zip(arriving, (span, span_two, span_three)):
        current = advance(current, incoming, reach)
    wire = current.astype(BF16)

    incoming = passed_along(wire, "tm", 4)
    begun, *factors = trailing_edge(strip, inverses, after(one_rows, wire), second_edge)
    passed_eight = passed_along(half_eight, "tm", 8)
    incoming, begun, half_eight = lax.optimization_barrier((incoming, begun, half_eight))
    current = advance(current, incoming, span_four)
    wire = current.astype(BF16)

    incoming = passed_along(wire, "tm", 8)
    other = lax.ppermute(after(own, wire), "blk", [(i, i ^ 1) for i in range(blocks)])
    span_eight = joined(after(half_eight, wire))
    half_sixteen = matmul_high(span_eight, passed_eight)
    incoming, half_sixteen = lax.optimization_barrier((incoming, half_sixteen))
    span_sixteen = joined(half_sixteen)
    current = advance(current, incoming, span_eight)
    wire = current.astype(BF16)

    incoming = passed_along(wire, "tm", 16)
    trailing = trailing_far(strip, begun, factors, factor_at_two, own, other)
    incoming, trailing = lax.optimization_barrier((incoming, trailing))
    current = advance(current, incoming, span_sixteen)
    return (trailing[None], current[None])


def solution(mesh):
    placed = (P("tm", "blk", None), P("tm", None, None, None), P("tm", None, None), P())
    return jax.shard_map(
        body,
        mesh=mesh,
        in_specs=placed,
        out_specs=(P("tm", "blk", None), P("tm", None, None)),
        check_vma=False,
    )
```

```python
import jax
import jax.numpy as jnp
from jax import lax
from jax.experimental.layout import Layout, with_layout_constraint
from jax.experimental import pallas as pl
from jax.experimental.pallas import tpu as pltpu
from jax.sharding import PartitionSpec as P

BF16 = jnp.bfloat16
F32 = jnp.float32
VMEM_BYTES = 16 << 20


def passed_along(x, axis, by):
    count = lax.axis_size(axis)
    return lax.ppermute(x, axis, [(i, i + by) for i in range(count - by)])


def core_passed(x, reaches):
    count, blocks = lax.axis_size("tm"), lax.axis_size("blk")
    pairs = [
        (i * blocks + j, (i + reaches[j % 2]) * blocks + j)
        for i in range(count)
        for j in range(blocks)
        if reaches[j % 2] and i + reaches[j % 2] < count
    ]
    return lax.ppermute(x, ("tm", "blk"), pairs)


def matmul_high(left, right):
    return jnp.dot(left, right, precision=lax.Precision.HIGHEST, preferred_element_type=F32)


def rounded_dot(left, right):
    return jnp.dot(left, right, preferred_element_type=F32).astype(BF16)


def reduced_by(block, factor, rows):
    product = jnp.dot(factor, rows, preferred_element_type=F32)
    return (block.astype(F32) - product).astype(BF16)


def pick_kernel(w, per, chunks, nodes_hbm, strip_hbm, near_ref, far_hbm, strip_ref, nodes_ref, far_ref, sems, far_sems):
    rows = strip_ref.shape[0]
    cols = strip_ref.shape[1] // chunks

    def part(i):
        at = pl.ds(i * cols, cols)
        return pltpu.make_async_copy(strip_hbm.at[:, at], strip_ref.at[:, at], sems.at[i])

    nodes = pltpu.make_async_copy(nodes_hbm, nodes_ref, sems.at[chunks])
    nodes.start()
    for i in [*range(1, chunks), 0]:
        part(i).start()
    nodes.wait()
    me = lax.axis_index("blk")
    lanes = 128
    at_row = lax.broadcasted_iota(jnp.int32, (3 * per, lanes), 0)
    at_lane = lax.broadcasted_iota(jnp.int32, (3 * per, lanes), 1)
    wanted = jnp.zeros((3 * per, lanes), jnp.int32)
    for k in range(3):
        for i in range(per):
            wanted = jnp.where(at_row == k * per + i, nodes_ref[k, me * per + i] - me * rows, wanted)
    picker = jnp.concatenate(
        [(wanted == at_lane + first).astype(F32).astype(BF16) for first in range(0, rows, lanes)], 1
    )
    width = far_ref.shape[2] // 2
    copies = []
    for i in [*range(1, chunks), 0]:
        part(i).wait()
        at = pl.ds(i * cols, cols)
        got = jnp.dot(picker, strip_ref[:, at], preferred_element_type=F32).astype(BF16)
        one, two, edge = got[:per], got[per:2 * per], got[2 * per:]
        if i == 0:
            near_ref[:, :2 * w] = one[:, w:]
            near_ref[:, 2 * w:3 * w] = two[:, :w]
            near_ref[:, 3 * w:4 * w] = two[:, 2 * w:]
            near_ref[:, 4 * w:] = edge
        else:
            far_ref[i - 1, :, :width] = one
            far_ref[i - 1, :, width:] = two
            for row in range((i - 1) * per, far_hbm.shape[0], 2 * per):
                copies.append(
                    pltpu.make_async_copy(
                        far_ref.at[i - 1], far_hbm.at[pl.ds(row, per), :], far_sems.at[row // per]
                    )
                )
                copies[-1].start()
    for copy in copies:
        copy.wait()


def picked_rows(pivot_nodes, strip, w, per):
    rows, width = strip.shape
    chunks = width // (3 * w)
    return pl.pallas_call(
        lambda *refs: pick_kernel(w, per, chunks, *refs),
        out_shape=(
            pltpu.VMEM((per, 7 * w), BF16),
            jax.ShapeDtypeStruct((w, width - 3 * w), BF16),
        ),
        in_specs=[pl.BlockSpec(memory_space=pltpu.HBM), pl.BlockSpec(memory_space=pltpu.HBM)],
        out_specs=(pl.BlockSpec(memory_space=pltpu.VMEM), pl.BlockSpec(memory_space=pl.ANY)),
        scratch_shapes=[
            pltpu.VMEM((rows, width), BF16),
            pltpu.SMEM(pivot_nodes.shape, jnp.int32),
            pltpu.VMEM((chunks - 1, per, width - 3 * w), BF16),
            pltpu.SemaphoreType.DMA((chunks + 1,)),
            pltpu.SemaphoreType.DMA((w // per,)),
        ],
        cost_estimate=pl.CostEstimate(
            flops=2 * 3 * per * rows * width, bytes_accessed=2 * rows * width, transcendentals=0
        ),
        name="pick",
    )(pivot_nodes, strip)


def boundary_kernel(w, near_ref, inverse_ref, boundary_ref, factor_ref, second_ref, ones_ref):
    near = near_ref[...]
    one_edge = near[:, w:2 * w]
    edge = near[:, 4 * w:]
    factor_at_two = rounded_dot(near[:, 2 * w:3 * w], inverse_ref[0])
    factor_at_edge = rounded_dot(edge[:, :w], inverse_ref[0])
    updated = reduced_by(edge[:, w:], factor_at_edge, near[:, :2 * w])
    second_edge = reduced_by(near[:, 3 * w:4 * w], factor_at_two, one_edge)
    factor_two = rounded_dot(updated[:, :w], inverse_ref[1])
    boundary_ref[...] = reduced_by(updated[:, w:], factor_two, second_edge)
    factor_ref[...] = factor_at_two
    second_ref[...] = second_edge
    ones_ref[...] = near[:, :2 * w]


def boundary_of(near, inverses):
    w = near.shape[0]
    block = pltpu.VMEM((w, w), BF16)
    near = pltpu.with_memory_space_constraint(near, pltpu.VMEM)
    vmem = pl.BlockSpec(memory_space=pltpu.VMEM)
    return pl.pallas_call(
        lambda *refs: boundary_kernel(w, *refs),
        out_shape=(block, block, block, pltpu.VMEM((w, 2 * w), BF16)),
        in_specs=[vmem, vmem],
        out_specs=(vmem, vmem, vmem, vmem),
        cost_estimate=pl.CostEstimate(flops=14 * w * w * w, bytes_accessed=12 * w * 2 * w, transcendentals=0),
        compiler_params=pltpu.CompilerParams(vmem_limit_bytes=VMEM_BYTES),
        name="boundary",
    )(near, inverses)


def edge_kernel(
    w, strip_hbm, inverse_ref, ones_ref, second_ref, out_hbm, one_ref, two_ref, strip_ref, edge_ref, sems
):
    def part(i):
        at = pl.ds(i * w, w)
        return pltpu.make_async_copy(strip_hbm.at[:, at], strip_ref.at[:, at], sems.at[i])

    for i in range(3):
        part(i).start()
    part(0).wait()
    one_ref[...] = rounded_dot(strip_ref[:, :w], inverse_ref[0])
    part(1).wait()
    panel = reduced_by(strip_ref[:, w:2 * w], one_ref[...], ones_ref[:, :w])
    two_ref[...] = rounded_dot(panel, inverse_ref[1])
    part(2).wait()
    updated = reduced_by(strip_ref[:, 2 * w:], one_ref[...], ones_ref[:, w:])
    edge_ref[...] = reduced_by(updated, two_ref[...], second_ref[...])
    done = pltpu.make_async_copy(edge_ref, out_hbm.at[:, pl.ds(0, w)], sems.at[3])
    done.start()
    done.wait()


def far_kernel(
    w, strip_hbm, begun_hbm, own_hbm, other_ref, one_ref, two_ref, factor_ref, out_hbm,
    strip_ref, own_ref, out_ref, sems, own_sem,
):
    del begun_hbm
    half = own_hbm.shape[1] // 2
    per_half = half // w
    count = 2 * per_half
    core = lax.rem(lax.axis_index("blk"), 2)

    blocks = [which * per_half + k for which in (core, 1 - core) for k in range(per_half)]

    def columns(block):
        return pl.ds(pl.multiple_of(block * w, w), w)

    def part(i):
        at = columns(blocks[i] + 3)
        return pltpu.make_async_copy(strip_hbm.at[:, at], strip_ref.at[:, i * w:(i + 1) * w], sems.at[0, i])

    def done_part(i):
        at = columns(blocks[i] + 1)
        return pltpu.make_async_copy(out_ref.at[:, i * w:(i + 1) * w], out_hbm.at[:, at], sems.at[1, i])

    own = pltpu.make_async_copy(own_hbm, own_ref, own_sem)
    own.start()
    for i in range(count):
        part(i).start()
    own.wait()
    for i in range(count):
        ref, k = (own_ref, i) if i < per_half else (other_ref, i - per_half)
        one_rows = ref[:, k * w:(k + 1) * w]
        two_rows = reduced_by(ref[:, half + k * w:half + (k + 1) * w], factor_ref[...], one_rows)
        part(i).wait()
        updated = reduced_by(strip_ref[:, i * w:(i + 1) * w], one_ref[...], one_rows)
        out_ref[:, i * w:(i + 1) * w] = reduced_by(updated, two_ref[...], two_rows)
        done_part(i).start()
    for i in range(count):
        done_part(i).wait()


def in_vmem(*arrays):
    return tuple(pltpu.with_memory_space_constraint(x, pltpu.VMEM) for x in arrays)


def trailing_edge(strip, inverses, ones, second_edge):
    rows, width = strip.shape
    w = ones.shape[0]
    vmem, hbm = pl.BlockSpec(memory_space=pltpu.VMEM), pl.BlockSpec(memory_space=pl.ANY)
    return pl.pallas_call(
        lambda *refs: edge_kernel(w, *refs),
        out_shape=(
            jax.ShapeDtypeStruct((rows, width - 2 * w), BF16),
            pltpu.VMEM((rows, w), BF16),
            pltpu.VMEM((rows, w), BF16),
        ),
        in_specs=[hbm, vmem, vmem, vmem],
        out_specs=(hbm, vmem, vmem),
        scratch_shapes=[
            pltpu.VMEM((rows, 3 * w), BF16),
            pltpu.VMEM((rows, w), BF16),
            pltpu.SemaphoreType.DMA((4,)),
        ],
        cost_estimate=pl.CostEstimate(
            flops=w, bytes_accessed=w, transcendentals=0
        ),
        name="edge",
    )(strip, inverses, *in_vmem(ones, second_edge))


def trailing_far(strip, begun, factors, factor_at_two, own, other):
    rows, width = strip.shape
    w = factor_at_two.shape[0]
    blocks = width // w - 3
    vmem, hbm = pl.BlockSpec(memory_space=pltpu.VMEM), pl.BlockSpec(memory_space=pl.ANY)
    return pl.pallas_call(
        lambda *refs: far_kernel(w, *refs),
        out_shape=jax.ShapeDtypeStruct(begun.shape, BF16),
        in_specs=[hbm] * 3 + [vmem] * 4,
        out_specs=hbm,
        input_output_aliases={1: 0},
        scratch_shapes=[
            pltpu.VMEM((rows, blocks * w), BF16),
            pltpu.VMEM(own.shape, BF16),
            pltpu.VMEM((rows, blocks * w), BF16),
            pltpu.SemaphoreType.DMA((2, blocks)),
            pltpu.SemaphoreType.DMA,
        ],
        cost_estimate=pl.CostEstimate(
            flops=w, bytes_accessed=w, transcendentals=0
        ),
        name="far",
    )(strip, begun, own, *in_vmem(other, *factors, factor_at_two))


def after(x, gate):
    return lax.optimization_barrier((x, gate))[0]


def body(panel_strip, pivot_inverses, coupling, pivot_nodes):
    strip = panel_strip[0]
    inverses = pivot_inverses[0]
    span = coupling[0]
    w = span.shape[0]
    blocks = lax.axis_size("blk")
    per = w // blocks

    back_one, back_two, back_three = (passed_along(span, "tm", by) for by in (1, 2, 3))

    near_here, far_here = picked_rows(pivot_nodes, strip, w, per)
    near = lax.all_gather(near_here, "blk", axis=0, tiled=True)
    near, far_here = lax.optimization_barrier((near, far_here))
    own = lax.all_to_all(far_here, "blk", 0, 0, tiled=True)
    boundary, factor_at_two, second_edge, one_rows = boundary_of(near, inverses)
    back_one, back_two, back_three, boundary = lax.optimization_barrier(
        (back_one, back_two, back_three, boundary)
    )

    def advance(current, incoming, reach):
        return matmul_high(matmul_high(reach, incoming.astype(F32)), reach.T) + current

    core_pairs = [[i, i + 1] for i in range(0, blocks, 2)]

    def joined(half):
        return lax.all_gather(half, "blk", axis=1, tiled=True, axis_index_groups=core_pairs)

    arriving = [core_passed(boundary, by) for by in ((1, 2), (3, None))]
    span_two = matmul_high(span, back_one)
    span_three = matmul_high(span_two, back_two)
    span_four = matmul_high(span_three, back_three)
    core = lax.axis_index("blk") % 2
    half_four = lax.dynamic_slice_in_dim(span_four, core * (w // 2), w // 2, 1)
    half_eight = matmul_high(span_four, passed_along(half_four, "tm", 4))
    terms = jnp.zeros((w, w), F32)
    by_core = with_layout_constraint(jnp.where(core == 0, span, span_two), Layout((0, 1)))
    for incoming, reach in zip(arriving, (by_core, span_three)):
        terms = advance(terms, incoming, reach)
    terms = lax.all_gather(terms, "blk", axis_index_groups=core_pairs)
    current = boundary.astype(F32) + (terms[0] + terms[1])
    wire = current.astype(BF16)

    incoming = passed_along(wire, "tm", 4)
    begun, *factors = trailing_edge(strip, inverses, after(one_rows, wire), second_edge)
    passed_eight = passed_along(half_eight, "tm", 8)
    incoming, begun, half_eight = lax.optimization_barrier((incoming, begun, half_eight))
    current = advance(current, incoming, span_four)
    wire = current.astype(BF16)

    incoming = passed_along(wire, "tm", 8)
    other = lax.ppermute(after(own, wire), "blk", [(i, i ^ 1) for i in range(blocks)])
    span_eight = joined(after(half_eight, wire))
    half_sixteen = matmul_high(span_eight, passed_eight)
    incoming, half_sixteen = lax.optimization_barrier((incoming, half_sixteen))
    span_sixteen = joined(half_sixteen)
    current = advance(current, incoming, span_eight)
    wire = current.astype(BF16)

    incoming = passed_along(wire, "tm", 16)
    trailing = trailing_far(strip, begun, factors, factor_at_two, own, other)
    incoming, trailing = lax.optimization_barrier((incoming, trailing))
    current = advance(current, incoming, span_sixteen)
    return (trailing[None], current[None])


def solution(mesh):
    placed = (P("tm", "blk", None), P("tm", None, None, None), P("tm", None, None), P())
    return jax.shard_map(
        body,
        mesh=mesh,
        in_specs=placed,
        out_specs=(P("tm", "blk", None), P("tm", None, None)),
        check_vma=False,
    )
```

```python
import jax
import jax.numpy as jnp
from jax import lax
from jax.experimental.layout import Layout, with_layout_constraint
from jax.experimental import pallas as pl
from jax.experimental.pallas import tpu as pltpu
from jax.sharding import PartitionSpec as P

BF16 = jnp.bfloat16
F32 = jnp.float32
VMEM_BYTES = 16 << 20


def passed_along(x, axis, by):
    count = lax.axis_size(axis)
    return lax.ppermute(x, axis, [(i, i + by) for i in range(count - by)])


def core_passed(x, reaches):
    count, blocks = lax.axis_size("tm"), lax.axis_size("blk")
    pairs = [
        (i * blocks + j, (i + reaches[j % 2]) * blocks + j)
        for i in range(count)
        for j in range(blocks)
        if reaches[j % 2] and i + reaches[j % 2] < count
    ]
    return lax.ppermute(x, ("tm", "blk"), pairs)


def matmul_high(left, right):
    return jnp.dot(left, right, precision=lax.Precision.HIGHEST, preferred_element_type=F32)


def rounded_dot(left, right):
    return jnp.dot(left, right, preferred_element_type=F32).astype(BF16)


def reduced_by(block, factor, rows):
    product = jnp.dot(factor, rows, preferred_element_type=F32)
    return (block.astype(F32) - product).astype(BF16)


def pick_kernel(w, per, chunks, nodes_hbm, strip_hbm, near_ref, far_hbm, strip_ref, nodes_ref, far_ref, sems, far_sems):
    rows = strip_ref.shape[0]
    cols = strip_ref.shape[1] // chunks

    def part(i):
        at = pl.ds(i * cols, cols)
        return pltpu.make_async_copy(strip_hbm.at[:, at], strip_ref.at[:, at], sems.at[i])

    nodes = pltpu.make_async_copy(nodes_hbm, nodes_ref, sems.at[chunks])
    nodes.start()
    for i in [*range(1, chunks), 0]:
        part(i).start()
    nodes.wait()
    me = lax.axis_index("blk")
    lanes = 128
    at_row = lax.broadcasted_iota(jnp.int32, (3 * per, lanes), 0)
    at_lane = lax.broadcasted_iota(jnp.int32, (3 * per, lanes), 1)
    wanted = jnp.zeros((3 * per, lanes), jnp.int32)
    for k in range(3):
        for i in range(per):
            wanted = jnp.where(at_row == k * per + i, nodes_ref[k, me * per + i] - me * rows, wanted)
    picker = jnp.concatenate(
        [(wanted == at_lane + first).astype(F32).astype(BF16) for first in range(0, rows, lanes)], 1
    )
    width = far_ref.shape[2] // 2
    copies = []
    for i in [*range(1, chunks), 0]:
        part(i).wait()
        at = pl.ds(i * cols, cols)
        got = jnp.dot(picker, strip_ref[:, at], preferred_element_type=F32).astype(BF16)
        one, two, edge = got[:per], got[per:2 * per], got[2 * per:]
        if i == 0:
            near_ref[:, :2 * w] = one[:, w:]
            near_ref[:, 2 * w:3 * w] = two[:, :w]
            near_ref[:, 3 * w:4 * w] = two[:, 2 * w:]
            near_ref[:, 4 * w:] = edge
        else:
            far_ref[i - 1, :, :width] = one
            far_ref[i - 1, :, width:] = two
            for row in range((i - 1) * per, far_hbm.shape[0], 2 * per):
                copies.append(
                    pltpu.make_async_copy(
                        far_ref.at[i - 1], far_hbm.at[pl.ds(row, per), :], far_sems.at[row // per]
                    )
                )
                copies[-1].start()
    for copy in copies:
        copy.wait()


def picked_rows(pivot_nodes, strip, w, per):
    rows, width = strip.shape
    chunks = width // (3 * w)
    return pl.pallas_call(
        lambda *refs: pick_kernel(w, per, chunks, *refs),
        out_shape=(
            pltpu.VMEM((per, 7 * w), BF16),
            jax.ShapeDtypeStruct((w, width - 3 * w), BF16),
        ),
        in_specs=[pl.BlockSpec(memory_space=pltpu.HBM), pl.BlockSpec(memory_space=pltpu.HBM)],
        out_specs=(pl.BlockSpec(memory_space=pltpu.VMEM), pl.BlockSpec(memory_space=pl.ANY)),
        scratch_shapes=[
            pltpu.VMEM((rows, width), BF16),
            pltpu.SMEM(pivot_nodes.shape, jnp.int32),
            pltpu.VMEM((chunks - 1, per, width - 3 * w), BF16),
            pltpu.SemaphoreType.DMA((chunks + 1,)),
            pltpu.SemaphoreType.DMA((w // per,)),
        ],
        cost_estimate=pl.CostEstimate(
            flops=2 * 3 * per * rows * width, bytes_accessed=2 * rows * width, transcendentals=0
        ),
        name="pick",
    )(pivot_nodes, strip)


def boundary_kernel(w, near_ref, inverse_ref, boundary_ref, factor_ref, second_ref, ones_ref):
    near = near_ref[...]
    one_edge = near[:, w:2 * w]
    edge = near[:, 4 * w:]
    factor_at_two = rounded_dot(near[:, 2 * w:3 * w], inverse_ref[0])
    factor_at_edge = rounded_dot(edge[:, :w], inverse_ref[0])
    updated = reduced_by(edge[:, w:], factor_at_edge, near[:, :2 * w])
    second_edge = reduced_by(near[:, 3 * w:4 * w], factor_at_two, one_edge)
    factor_two = rounded_dot(updated[:, :w], inverse_ref[1])
    boundary_ref[...] = reduced_by(updated[:, w:], factor_two, second_edge)
    factor_ref[...] = factor_at_two
    second_ref[...] = second_edge
    ones_ref[...] = near[:, :2 * w]


def boundary_of(near, inverses):
    w = near.shape[0]
    block = pltpu.VMEM((w, w), BF16)
    near = pltpu.with_memory_space_constraint(near, pltpu.VMEM)
    vmem = pl.BlockSpec(memory_space=pltpu.VMEM)
    return pl.pallas_call(
        lambda *refs: boundary_kernel(w, *refs),
        out_shape=(block, block, block, pltpu.VMEM((w, 2 * w), BF16)),
        in_specs=[vmem, vmem],
        out_specs=(vmem, vmem, vmem, vmem),
        cost_estimate=pl.CostEstimate(flops=14 * w * w * w, bytes_accessed=12 * w * 2 * w, transcendentals=0),
        compiler_params=pltpu.CompilerParams(vmem_limit_bytes=VMEM_BYTES),
        name="boundary",
    )(near, inverses)


def edge_kernel(
    w, strip_hbm, inverse_ref, ones_ref, second_ref, out_hbm, one_ref, two_ref, strip_ref, edge_ref, sems
):
    def part(i):
        at = pl.ds(i * w, w)
        return pltpu.make_async_copy(strip_hbm.at[:, at], strip_ref.at[:, at], sems.at[i])

    for i in range(3):
        part(i).start()
    part(0).wait()
    one_ref[...] = rounded_dot(strip_ref[:, :w], inverse_ref[0])
    part(1).wait()
    panel = reduced_by(strip_ref[:, w:2 * w], one_ref[...], ones_ref[:, :w])
    two_ref[...] = rounded_dot(panel, inverse_ref[1])
    part(2).wait()
    updated = reduced_by(strip_ref[:, 2 * w:], one_ref[...], ones_ref[:, w:])
    edge_ref[...] = reduced_by(updated, two_ref[...], second_ref[...])
    done = pltpu.make_async_copy(edge_ref, out_hbm.at[:, pl.ds(0, w)], sems.at[3])
    done.start()
    done.wait()


def far_kernel(
    w, swap, strip_hbm, begun_hbm, far_ref, one_ref, two_ref, factor_ref, out_hbm, strip_ref, out_ref, sems
):
    del begun_hbm
    half = far_ref.shape[1] // 2
    count = half // w
    core = lax.rem(lax.axis_index("blk"), 2)
    which = 1 - core if swap else core

    def columns(block):
        return pl.ds(pl.multiple_of((which * count + block) * w, w), w)

    def part(i):
        at = columns(i + 3)
        return pltpu.make_async_copy(strip_hbm.at[:, at], strip_ref.at[:, i * w:(i + 1) * w], sems.at[0, i])

    def done_part(i):
        at = columns(i + 1)
        return pltpu.make_async_copy(out_ref.at[:, i * w:(i + 1) * w], out_hbm.at[:, at], sems.at[1, i])

    for i in range(count):
        part(i).start()
    for i in range(count):
        one_rows = far_ref[:, i * w:(i + 1) * w]
        two_rows = reduced_by(far_ref[:, half + i * w:half + (i + 1) * w], factor_ref[...], one_rows)
        part(i).wait()
        updated = reduced_by(strip_ref[:, i * w:(i + 1) * w], one_ref[...], one_rows)
        out_ref[:, i * w:(i + 1) * w] = reduced_by(updated, two_ref[...], two_rows)
        done_part(i).start()
    for i in range(count):
        done_part(i).wait()


def in_vmem(*arrays):
    return tuple(pltpu.with_memory_space_constraint(x, pltpu.VMEM) for x in arrays)


def trailing_edge(strip, inverses, ones, second_edge):
    rows, width = strip.shape
    w = ones.shape[0]
    vmem, hbm = pl.BlockSpec(memory_space=pltpu.VMEM), pl.BlockSpec(memory_space=pl.ANY)
    return pl.pallas_call(
        lambda *refs: edge_kernel(w, *refs),
        out_shape=(
            jax.ShapeDtypeStruct((rows, width - 2 * w), BF16),
            pltpu.VMEM((rows, w), BF16),
            pltpu.VMEM((rows, w), BF16),
        ),
        in_specs=[hbm, vmem, vmem, vmem],
        out_specs=(hbm, vmem, vmem),
        scratch_shapes=[
            pltpu.VMEM((rows, 3 * w), BF16),
            pltpu.VMEM((rows, w), BF16),
            pltpu.SemaphoreType.DMA((4,)),
        ],
        cost_estimate=pl.CostEstimate(
            flops=w, bytes_accessed=w, transcendentals=0
        ),
        name="edge",
    )(strip, inverses, *in_vmem(ones, second_edge))


def trailing_far(strip, begun, far, factors, factor_at_two, swap):
    rows = strip.shape[0]
    w = factor_at_two.shape[0]
    half = far.shape[1] // 2
    vmem, hbm = pl.BlockSpec(memory_space=pltpu.VMEM), pl.BlockSpec(memory_space=pl.ANY)
    return pl.pallas_call(
        lambda *refs: far_kernel(w, swap, *refs),
        out_shape=jax.ShapeDtypeStruct(begun.shape, BF16),
        in_specs=[hbm] * 2 + [vmem] * 4,
        out_specs=hbm,
        input_output_aliases={1: 0},
        scratch_shapes=[
            pltpu.VMEM((rows, half), BF16),
            pltpu.VMEM((rows, half), BF16),
            pltpu.SemaphoreType.DMA((2, half // w)),
        ],
        cost_estimate=pl.CostEstimate(
            flops=w, bytes_accessed=w, transcendentals=0
        ),
        name="far_swapped" if swap else "far",
    )(strip, begun, *in_vmem(far, *factors, factor_at_two))


def after(x, gate):
    return lax.optimization_barrier((x, gate))[0]


def body(panel_strip, pivot_inverses, coupling, pivot_nodes):
    strip = panel_strip[0]
    inverses = pivot_inverses[0]
    span = coupling[0]
    w = span.shape[0]
    blocks = lax.axis_size("blk")
    per = w // blocks

    back_one, back_two, back_three = (passed_along(span, "tm", by) for by in (1, 2, 3))

    near_here, far_here = picked_rows(pivot_nodes, strip, w, per)
    near = lax.all_gather(near_here, "blk", axis=0, tiled=True)
    near, far_here = lax.optimization_barrier((near, far_here))
    own = lax.all_to_all(far_here, "blk", 0, 0, tiled=True)
    boundary, factor_at_two, second_edge, one_rows = boundary_of(near, inverses)
    back_one, back_two, back_three, boundary = lax.optimization_barrier(
        (back_one, back_two, back_three, boundary)
    )

    def advance(current, incoming, reach):
        return matmul_high(matmul_high(reach, incoming.astype(F32)), reach.T) + current

    core_pairs = [[i, i + 1] for i in range(0, blocks, 2)]

    def joined(half):
        return lax.all_gather(half, "blk", axis=1, tiled=True, axis_index_groups=core_pairs)

    arriving = [core_passed(boundary, by) for by in ((1, 2), (3, None))]
    span_two = matmul_high(span, back_one)
    span_three = matmul_high(span_two, back_two)
    span_four = matmul_high(span_three, back_three)
    core = lax.axis_index("blk") % 2
    half_four = lax.dynamic_slice_in_dim(span_four, core * (w // 2), w // 2, 1)
    half_eight = matmul_high(span_four, passed_along(half_four, "tm", 4))
    terms = jnp.zeros((w, w), F32)
    by_core = with_layout_constraint(jnp.where(core == 0, span, span_two), Layout((0, 1)))
    for incoming, reach in zip(arriving, (by_core, span_three)):
        terms = advance(terms, incoming, reach)
    terms = lax.all_gather(terms, "blk", axis_index_groups=core_pairs)
    current = boundary.astype(F32) + (terms[0] + terms[1])
    wire = current.astype(BF16)

    incoming = passed_along(wire, "tm", 4)
    begun, *factors = trailing_edge(strip, inverses, after(one_rows, wire), second_edge)
    passed_eight = passed_along(half_eight, "tm", 8)
    incoming, begun, half_eight = lax.optimization_barrier((incoming, begun, half_eight))
    current = advance(current, incoming, span_four)
    wire = current.astype(BF16)

    incoming = passed_along(wire, "tm", 8)
    own = after(own, wire)
    other = lax.ppermute(own, "blk", [(i, i ^ 1) for i in range(blocks)])
    trailing = trailing_far(strip, begun, own, factors, factor_at_two, False)
    span_eight = joined(after(half_eight, wire))
    half_sixteen = matmul_high(span_eight, passed_eight)
    incoming, half_sixteen, trailing = lax.optimization_barrier((incoming, half_sixteen, trailing))
    span_sixteen = joined(half_sixteen)
    current = advance(current, incoming, span_eight)
    wire = current.astype(BF16)

    incoming = passed_along(wire, "tm", 16)
    trailing = trailing_far(strip, trailing, other, factors, factor_at_two, True)
    incoming, trailing = lax.optimization_barrier((incoming, trailing))
    current = advance(current, incoming, span_sixteen)
    return (trailing[None], current[None])


def solution(mesh):
    placed = (P("tm", "blk", None), P("tm", None, None, None), P("tm", None, None), P())
    return jax.shard_map(
        body,
        mesh=mesh,
        in_specs=placed,
        out_specs=(P("tm", "blk", None), P("tm", None, None)),
        check_vma=False,
    )
```

```python
import jax
import jax.numpy as jnp
from jax import lax
from jax.experimental.layout import Layout, with_layout_constraint
from jax.experimental import pallas as pl
from jax.experimental.pallas import tpu as pltpu
from jax.sharding import PartitionSpec as P

BF16 = jnp.bfloat16
F32 = jnp.float32
VMEM_BYTES = 16 << 20


def passed_along(x, axis, by):
    count = lax.axis_size(axis)
    return lax.ppermute(x, axis, [(i, i + by) for i in range(count - by)])


def core_passed(x, reaches):
    count, blocks = lax.axis_size("tm"), lax.axis_size("blk")
    pairs = [
        (i * blocks + j, (i + reaches[j % 2]) * blocks + j)
        for i in range(count)
        for j in range(blocks)
        if reaches[j % 2] and i + reaches[j % 2] < count
    ]
    return lax.ppermute(x, ("tm", "blk"), pairs)


def matmul_high(left, right):
    return jnp.dot(left, right, precision=lax.Precision.HIGHEST, preferred_element_type=F32)


def rounded_dot(left, right):
    return jnp.dot(left, right, preferred_element_type=F32).astype(BF16)


def reduced_by(block, factor, rows):
    product = jnp.dot(factor, rows, preferred_element_type=F32)
    return (block.astype(F32) - product).astype(BF16)


def pick_kernel(w, per, chunks, nodes_hbm, strip_hbm, near_ref, far_hbm, strip_ref, nodes_ref, far_ref, sems, far_sems):
    rows = strip_ref.shape[0]
    cols = strip_ref.shape[1] // chunks

    def part(i):
        at = pl.ds(i * cols, cols)
        return pltpu.make_async_copy(strip_hbm.at[:, at], strip_ref.at[:, at], sems.at[i])

    nodes = pltpu.make_async_copy(nodes_hbm, nodes_ref, sems.at[chunks])
    nodes.start()
    for i in [*range(1, chunks), 0]:
        part(i).start()
    nodes.wait()
    me = lax.axis_index("blk")
    lanes = 128
    at_row = lax.broadcasted_iota(jnp.int32, (3 * per, lanes), 0)
    at_lane = lax.broadcasted_iota(jnp.int32, (3 * per, lanes), 1)
    wanted = jnp.zeros((3 * per, lanes), jnp.int32)
    for k in range(3):
        for i in range(per):
            wanted = jnp.where(at_row == k * per + i, nodes_ref[k, me * per + i] - me * rows, wanted)
    picker = jnp.concatenate(
        [(wanted == at_lane + first).astype(F32).astype(BF16) for first in range(0, rows, lanes)], 1
    )
    width = far_ref.shape[2] // 2
    copies = []
    for i in [*range(1, chunks), 0]:
        part(i).wait()
        at = pl.ds(i * cols, cols)
        got = jnp.dot(picker, strip_ref[:, at], preferred_element_type=F32).astype(BF16)
        one, two, edge = got[:per], got[per:2 * per], got[2 * per:]
        if i == 0:
            near_ref[:, :2 * w] = one[:, w:]
            near_ref[:, 2 * w:3 * w] = two[:, :w]
            near_ref[:, 3 * w:4 * w] = two[:, 2 * w:]
            near_ref[:, 4 * w:] = edge
        else:
            far_ref[i - 1, :, :width] = one
            far_ref[i - 1, :, width:] = two
            for row in range((i - 1) * per, far_hbm.shape[0], 2 * per):
                copies.append(
                    pltpu.make_async_copy(
                        far_ref.at[i - 1], far_hbm.at[pl.ds(row, per), :], far_sems.at[row // per]
                    )
                )
                copies[-1].start()
    for copy in copies:
        copy.wait()


def picked_rows(pivot_nodes, strip, w, per):
    rows, width = strip.shape
    chunks = width // (3 * w)
    return pl.pallas_call(
        lambda *refs: pick_kernel(w, per, chunks, *refs),
        out_shape=(
            pltpu.VMEM((per, 7 * w), BF16),
            jax.ShapeDtypeStruct((w, width - 3 * w), BF16),
        ),
        in_specs=[pl.BlockSpec(memory_space=pltpu.HBM), pl.BlockSpec(memory_space=pltpu.HBM)],
        out_specs=(pl.BlockSpec(memory_space=pltpu.VMEM), pl.BlockSpec(memory_space=pl.ANY)),
        scratch_shapes=[
            pltpu.VMEM((rows, width), BF16),
            pltpu.SMEM(pivot_nodes.shape, jnp.int32),
            pltpu.VMEM((chunks - 1, per, width - 3 * w), BF16),
            pltpu.SemaphoreType.DMA((chunks + 1,)),
            pltpu.SemaphoreType.DMA((w // per,)),
        ],
        cost_estimate=pl.CostEstimate(
            flops=2 * 3 * per * rows * width, bytes_accessed=2 * rows * width, transcendentals=0
        ),
        name="pick",
    )(pivot_nodes, strip)


def boundary_kernel(w, near_ref, inverse_ref, boundary_ref, factor_ref, second_ref, ones_ref):
    near = near_ref[...]
    one_edge = near[:, w:2 * w]
    edge = near[:, 4 * w:]
    factor_at_two = rounded_dot(near[:, 2 * w:3 * w], inverse_ref[0])
    factor_at_edge = rounded_dot(edge[:, :w], inverse_ref[0])
    updated = reduced_by(edge[:, w:], factor_at_edge, near[:, :2 * w])
    second_edge = reduced_by(near[:, 3 * w:4 * w], factor_at_two, one_edge)
    factor_two = rounded_dot(updated[:, :w], inverse_ref[1])
    boundary_ref[...] = reduced_by(updated[:, w:], factor_two, second_edge)
    factor_ref[...] = factor_at_two
    second_ref[...] = second_edge
    ones_ref[...] = near[:, :2 * w]


def boundary_of(near, inverses):
    w = near.shape[0]
    block = pltpu.VMEM((w, w), BF16)
    near = pltpu.with_memory_space_constraint(near, pltpu.VMEM)
    vmem = pl.BlockSpec(memory_space=pltpu.VMEM)
    return pl.pallas_call(
        lambda *refs: boundary_kernel(w, *refs),
        out_shape=(block, block, block, pltpu.VMEM((w, 2 * w), BF16)),
        in_specs=[vmem, vmem],
        out_specs=(vmem, vmem, vmem, vmem),
        cost_estimate=pl.CostEstimate(flops=14 * w * w * w, bytes_accessed=12 * w * 2 * w, transcendentals=0),
        compiler_params=pltpu.CompilerParams(vmem_limit_bytes=VMEM_BYTES),
        name="boundary",
    )(near, inverses)


def edge_kernel(
    w, strip_hbm, inverse_ref, ones_ref, second_ref, out_hbm, one_ref, two_ref, strip_ref, edge_ref, sems
):
    def part(i):
        at = pl.ds(i * w, w)
        return pltpu.make_async_copy(strip_hbm.at[:, at], strip_ref.at[:, at], sems.at[i])

    for i in range(3):
        part(i).start()
    part(0).wait()
    one_ref[...] = rounded_dot(strip_ref[:, :w], inverse_ref[0])
    part(1).wait()
    panel = reduced_by(strip_ref[:, w:2 * w], one_ref[...], ones_ref[:, :w])
    two_ref[...] = rounded_dot(panel, inverse_ref[1])
    part(2).wait()
    updated = reduced_by(strip_ref[:, 2 * w:], one_ref[...], ones_ref[:, w:])
    edge_ref[...] = reduced_by(updated, two_ref[...], second_ref[...])
    done = pltpu.make_async_copy(edge_ref, out_hbm.at[:, pl.ds(0, w)], sems.at[3])
    done.start()
    done.wait()


def far_kernel(
    w, swap, strip_hbm, begun_hbm, far_hbm, one_ref, two_ref, factor_ref, out_hbm,
    strip_ref, far_ref, out_ref, sems, far_sem,
):
    del begun_hbm
    half = far_ref.shape[1] // 2
    count = half // w
    core = lax.rem(lax.axis_index("blk"), 2)
    which = 1 - core if swap else core

    def columns(block):
        return pl.ds(pl.multiple_of((which * count + block) * w, w), w)

    def part(i):
        at = columns(i + 3)
        return pltpu.make_async_copy(strip_hbm.at[:, at], strip_ref.at[:, i * w:(i + 1) * w], sems.at[0, i])

    def done_part(i):
        at = columns(i + 1)
        return pltpu.make_async_copy(out_ref.at[:, i * w:(i + 1) * w], out_hbm.at[:, at], sems.at[1, i])

    far = pltpu.make_async_copy(far_hbm, far_ref, far_sem)
    far.start()
    for i in range(count):
        part(i).start()
    far.wait()
    for i in range(count):
        one_rows = far_ref[:, i * w:(i + 1) * w]
        two_rows = reduced_by(far_ref[:, half + i * w:half + (i + 1) * w], factor_ref[...], one_rows)
        part(i).wait()
        updated = reduced_by(strip_ref[:, i * w:(i + 1) * w], one_ref[...], one_rows)
        out_ref[:, i * w:(i + 1) * w] = reduced_by(updated, two_ref[...], two_rows)
        done_part(i).start()
    for i in range(count):
        done_part(i).wait()


def in_vmem(*arrays):
    return tuple(pltpu.with_memory_space_constraint(x, pltpu.VMEM) for x in arrays)


def trailing_edge(strip, inverses, ones, second_edge):
    rows, width = strip.shape
    w = ones.shape[0]
    vmem, hbm = pl.BlockSpec(memory_space=pltpu.VMEM), pl.BlockSpec(memory_space=pl.ANY)
    return pl.pallas_call(
        lambda *refs: edge_kernel(w, *refs),
        out_shape=(
            jax.ShapeDtypeStruct((rows, width - 2 * w), BF16),
            pltpu.VMEM((rows, w), BF16),
            pltpu.VMEM((rows, w), BF16),
        ),
        in_specs=[hbm, vmem, vmem, vmem],
        out_specs=(hbm, vmem, vmem),
        scratch_shapes=[
            pltpu.VMEM((rows, 3 * w), BF16),
            pltpu.VMEM((rows, w), BF16),
            pltpu.SemaphoreType.DMA((4,)),
        ],
        cost_estimate=pl.CostEstimate(
            flops=w, bytes_accessed=w, transcendentals=0
        ),
        name="edge",
    )(strip, inverses, *in_vmem(ones, second_edge))


def trailing_far(strip, begun, far, factors, factor_at_two, swap):
    rows = strip.shape[0]
    w = factor_at_two.shape[0]
    half = far.shape[1] // 2
    vmem, hbm = pl.BlockSpec(memory_space=pltpu.VMEM), pl.BlockSpec(memory_space=pl.ANY)
    return pl.pallas_call(
        lambda *refs: far_kernel(w, swap, *refs),
        out_shape=jax.ShapeDtypeStruct(begun.shape, BF16),
        in_specs=[hbm] * 3 + [vmem] * 3,
        out_specs=hbm,
        input_output_aliases={1: 0},
        scratch_shapes=[
            pltpu.VMEM((rows, half), BF16),
            pltpu.VMEM(far.shape, BF16),
            pltpu.VMEM((rows, half), BF16),
            pltpu.SemaphoreType.DMA((2, half // w)),
            pltpu.SemaphoreType.DMA,
        ],
        cost_estimate=pl.CostEstimate(
            flops=w, bytes_accessed=w, transcendentals=0
        ),
        name="far_swapped" if swap else "far",
    )(strip, begun, far, *in_vmem(*factors, factor_at_two))


def after(x, gate):
    return lax.optimization_barrier((x, gate))[0]


def body(panel_strip, pivot_inverses, coupling, pivot_nodes):
    strip = panel_strip[0]
    inverses = pivot_inverses[0]
    span = coupling[0]
    w = span.shape[0]
    blocks = lax.axis_size("blk")
    per = w // blocks

    back_one, back_two, back_three = (passed_along(span, "tm", by) for by in (1, 2, 3))

    near_here, far_here = picked_rows(pivot_nodes, strip, w, per)
    near = lax.all_gather(near_here, "blk", axis=0, tiled=True)
    near, far_here = lax.optimization_barrier((near, far_here))
    own = lax.all_to_all(far_here, "blk", 0, 0, tiled=True)
    boundary, factor_at_two, second_edge, one_rows = boundary_of(near, inverses)
    back_one, back_two, back_three, boundary = lax.optimization_barrier(
        (back_one, back_two, back_three, boundary)
    )

    def advance(current, incoming, reach):
        return matmul_high(matmul_high(reach, incoming.astype(F32)), reach.T) + current

    core_pairs = [[i, i + 1] for i in range(0, blocks, 2)]

    def joined(half):
        return lax.all_gather(half, "blk", axis=1, tiled=True, axis_index_groups=core_pairs)

    arriving = [core_passed(boundary, by) for by in ((3, 2), (1, None))]
    span_two = matmul_high(span, back_one)
    span_three = matmul_high(span_two, back_two)
    span_four = matmul_high(span_three, back_three)
    core = lax.axis_index("blk") % 2
    half_four = lax.dynamic_slice_in_dim(span_four, core * (w // 2), w // 2, 1)
    half_eight = matmul_high(span_four, passed_along(half_four, "tm", 4))
    terms = jnp.zeros((w, w), F32)
    by_core = with_layout_constraint(jnp.where(core == 0, span_three, span_two), Layout((0, 1)))
    for incoming, reach in zip(arriving, (by_core, span)):
        terms = advance(terms, incoming, reach)
    terms = lax.all_gather(terms, "blk", axis_index_groups=core_pairs)
    current = boundary.astype(F32) + (terms[0] + terms[1])
    wire = current.astype(BF16)

    incoming = passed_along(wire, "tm", 4)
    begun, *factors = trailing_edge(strip, inverses, after(one_rows, wire), second_edge)
    passed_eight = passed_along(half_eight, "tm", 8)
    incoming, begun, half_eight = lax.optimization_barrier((incoming, begun, half_eight))
    current = advance(current, incoming, span_four)
    wire = current.astype(BF16)

    incoming = passed_along(wire, "tm", 8)
    own = after(own, wire)
    other = lax.ppermute(own, "blk", [(i, i ^ 1) for i in range(blocks)])
    trailing = trailing_far(strip, begun, own, factors, factor_at_two, False)
    span_eight = joined(after(half_eight, wire))
    half_sixteen = matmul_high(span_eight, passed_eight)
    incoming, half_sixteen, trailing = lax.optimization_barrier((incoming, half_sixteen, trailing))
    span_sixteen = joined(half_sixteen)
    current = advance(current, incoming, span_eight)
    wire = current.astype(BF16)

    incoming = passed_along(wire, "tm", 16)
    trailing = trailing_far(strip, trailing, other, factors, factor_at_two, True)
    incoming, trailing = lax.optimization_barrier((incoming, trailing))
    current = advance(current, incoming, span_sixteen)
    return (trailing[None], current[None])


def solution(mesh):
    placed = (P("tm", "blk", None), P("tm", None, None, None), P("tm", None, None), P())
    return jax.shard_map(
        body,
        mesh=mesh,
        in_specs=placed,
        out_specs=(P("tm", "blk", None), P("tm", None, None)),
        check_vma=False,
    )
```

```python
import jax
import jax.numpy as jnp
from jax import lax
from jax.experimental.layout import Layout, with_layout_constraint
from jax.experimental import pallas as pl
from jax.experimental.pallas import tpu as pltpu
from jax.sharding import PartitionSpec as P

BF16 = jnp.bfloat16
F32 = jnp.float32
VMEM_BYTES = 16 << 20


def passed_along(x, axis, by):
    count = lax.axis_size(axis)
    return lax.ppermute(x, axis, [(i, i + by) for i in range(count - by)])


def core_passed(x, reaches):
    count, blocks = lax.axis_size("tm"), lax.axis_size("blk")
    pairs = [
        (i * blocks + j, (i + reaches[j % 2]) * blocks + j)
        for i in range(count)
        for j in range(blocks)
        if reaches[j % 2] and i + reaches[j % 2] < count
    ]
    return lax.ppermute(x, ("tm", "blk"), pairs)


def matmul_high(left, right):
    return jnp.dot(left, right, precision=lax.Precision.HIGHEST, preferred_element_type=F32)


def rounded_dot(left, right):
    return jnp.dot(left, right, preferred_element_type=F32).astype(BF16)


def reduced_by(block, factor, rows):
    product = jnp.dot(factor, rows, preferred_element_type=F32)
    return (block.astype(F32) - product).astype(BF16)


def pick_kernel(w, per, chunks, nodes_hbm, strip_hbm, near_ref, far_hbm, strip_ref, nodes_ref, far_ref, sems, far_sems):
    rows = strip_ref.shape[0]
    cols = strip_ref.shape[1] // chunks

    def part(i):
        at = pl.ds(i * cols, cols)
        return pltpu.make_async_copy(strip_hbm.at[:, at], strip_ref.at[:, at], sems.at[i])

    nodes = pltpu.make_async_copy(nodes_hbm, nodes_ref, sems.at[chunks])
    nodes.start()
    for i in [*range(1, chunks), 0]:
        part(i).start()
    nodes.wait()
    me = lax.axis_index("blk")
    lanes = 128
    at_row = lax.broadcasted_iota(jnp.int32, (3 * per, lanes), 0)
    at_lane = lax.broadcasted_iota(jnp.int32, (3 * per, lanes), 1)
    wanted = jnp.zeros((3 * per, lanes), jnp.int32)
    for k in range(3):
        for i in range(per):
            wanted = jnp.where(at_row == k * per + i, nodes_ref[k, me * per + i] - me * rows, wanted)
    picker = jnp.concatenate(
        [(wanted == at_lane + first).astype(F32).astype(BF16) for first in range(0, rows, lanes)], 1
    )
    width = far_ref.shape[2] // 2
    copies = []
    for i in [*range(1, chunks), 0]:
        part(i).wait()
        at = pl.ds(i * cols, cols)
        got = jnp.dot(picker, strip_ref[:, at], preferred_element_type=F32).astype(BF16)
        one, two, edge = got[:per], got[per:2 * per], got[2 * per:]
        if i == 0:
            near_ref[:, :2 * w] = one[:, w:]
            near_ref[:, 2 * w:3 * w] = two[:, :w]
            near_ref[:, 3 * w:4 * w] = two[:, 2 * w:]
            near_ref[:, 4 * w:] = edge
        else:
            far_ref[i - 1, :, :width] = one
            far_ref[i - 1, :, width:] = two
            for row in range((i - 1) * per, far_hbm.shape[0], 2 * per):
                copies.append(
                    pltpu.make_async_copy(
                        far_ref.at[i - 1], far_hbm.at[pl.ds(row, per), :], far_sems.at[row // per]
                    )
                )
                copies[-1].start()
    for copy in copies:
        copy.wait()


def picked_rows(pivot_nodes, strip, w, per):
    rows, width = strip.shape
    chunks = width // (3 * w)
    return pl.pallas_call(
        lambda *refs: pick_kernel(w, per, chunks, *refs),
        out_shape=(
            pltpu.VMEM((per, 7 * w), BF16),
            jax.ShapeDtypeStruct((w, width - 3 * w), BF16),
        ),
        in_specs=[pl.BlockSpec(memory_space=pltpu.HBM), pl.BlockSpec(memory_space=pltpu.HBM)],
        out_specs=(pl.BlockSpec(memory_space=pltpu.VMEM), pl.BlockSpec(memory_space=pl.ANY)),
        scratch_shapes=[
            pltpu.VMEM((rows, width), BF16),
            pltpu.SMEM(pivot_nodes.shape, jnp.int32),
            pltpu.VMEM((chunks - 1, per, width - 3 * w), BF16),
            pltpu.SemaphoreType.DMA((chunks + 1,)),
            pltpu.SemaphoreType.DMA((w // per,)),
        ],
        cost_estimate=pl.CostEstimate(
            flops=2 * 3 * per * rows * width, bytes_accessed=2 * rows * width, transcendentals=0
        ),
        name="pick",
    )(pivot_nodes, strip)


def boundary_kernel(w, near_ref, inverse_ref, boundary_ref, factor_ref, second_ref, ones_ref):
    near = near_ref[...]
    one_edge = near[:, w:2 * w]
    edge = near[:, 4 * w:]
    factor_at_two = rounded_dot(near[:, 2 * w:3 * w], inverse_ref[0])
    factor_at_edge = rounded_dot(edge[:, :w], inverse_ref[0])
    updated = reduced_by(edge[:, w:], factor_at_edge, near[:, :2 * w])
    second_edge = reduced_by(near[:, 3 * w:4 * w], factor_at_two, one_edge)
    factor_two = rounded_dot(updated[:, :w], inverse_ref[1])
    boundary_ref[...] = reduced_by(updated[:, w:], factor_two, second_edge)
    factor_ref[...] = factor_at_two
    second_ref[...] = second_edge
    ones_ref[...] = near[:, :2 * w]


def boundary_of(near, inverses):
    w = near.shape[0]
    block = pltpu.VMEM((w, w), BF16)
    near = pltpu.with_memory_space_constraint(near, pltpu.VMEM)
    vmem = pl.BlockSpec(memory_space=pltpu.VMEM)
    return pl.pallas_call(
        lambda *refs: boundary_kernel(w, *refs),
        out_shape=(block, block, block, pltpu.VMEM((w, 2 * w), BF16)),
        in_specs=[vmem, vmem],
        out_specs=(vmem, vmem, vmem, vmem),
        cost_estimate=pl.CostEstimate(flops=14 * w * w * w, bytes_accessed=12 * w * 2 * w, transcendentals=0),
        compiler_params=pltpu.CompilerParams(vmem_limit_bytes=VMEM_BYTES),
        name="boundary",
    )(near, inverses)


def edge_kernel(
    w, strip_hbm, inverse_ref, ones_ref, second_ref, out_hbm, one_ref, two_ref, strip_ref, edge_ref, sems
):
    def part(i):
        at = pl.ds(i * w, w)
        return pltpu.make_async_copy(strip_hbm.at[:, at], strip_ref.at[:, at], sems.at[i])

    for i in range(3):
        part(i).start()
    part(0).wait()
    one_ref[...] = rounded_dot(strip_ref[:, :w], inverse_ref[0])
    part(1).wait()
    panel = reduced_by(strip_ref[:, w:2 * w], one_ref[...], ones_ref[:, :w])
    two_ref[...] = rounded_dot(panel, inverse_ref[1])
    part(2).wait()
    updated = reduced_by(strip_ref[:, 2 * w:], one_ref[...], ones_ref[:, w:])
    edge_ref[...] = reduced_by(updated, two_ref[...], second_ref[...])
    done = pltpu.make_async_copy(edge_ref, out_hbm.at[:, pl.ds(0, w)], sems.at[3])
    done.start()
    done.wait()


def far_kernel(
    w, swap, strip_hbm, begun_hbm, far_ref, one_ref, two_ref, factor_ref, out_hbm, strip_ref, out_ref, sems
):
    del begun_hbm
    half = far_ref.shape[1] // 2
    count = half // w
    core = lax.rem(lax.axis_index("blk"), 2)
    which = 1 - core if swap else core

    def columns(block):
        return pl.ds(pl.multiple_of((which * count + block) * w, w), w)

    def part(i):
        at = columns(i + 3)
        return pltpu.make_async_copy(strip_hbm.at[:, at], strip_ref.at[:, i * w:(i + 1) * w], sems.at[0, i])

    def done_part(i):
        at = columns(i + 1)
        return pltpu.make_async_copy(out_ref.at[:, i * w:(i + 1) * w], out_hbm.at[:, at], sems.at[1, i])

    for i in range(count):
        part(i).start()
    for i in range(count):
        one_rows = far_ref[:, i * w:(i + 1) * w]
        two_rows = reduced_by(far_ref[:, half + i * w:half + (i + 1) * w], factor_ref[...], one_rows)
        part(i).wait()
        updated = reduced_by(strip_ref[:, i * w:(i + 1) * w], one_ref[...], one_rows)
        out_ref[:, i * w:(i + 1) * w] = reduced_by(updated, two_ref[...], two_rows)
        done_part(i).start()
    for i in range(count):
        done_part(i).wait()


def in_vmem(*arrays):
    return tuple(pltpu.with_memory_space_constraint(x, pltpu.VMEM) for x in arrays)


def trailing_edge(strip, inverses, ones, second_edge):
    rows, width = strip.shape
    w = ones.shape[0]
    vmem, hbm = pl.BlockSpec(memory_space=pltpu.VMEM), pl.BlockSpec(memory_space=pl.ANY)
    return pl.pallas_call(
        lambda *refs: edge_kernel(w, *refs),
        out_shape=(
            jax.ShapeDtypeStruct((rows, width - 2 * w), BF16),
            pltpu.VMEM((rows, w), BF16),
            pltpu.VMEM((rows, w), BF16),
        ),
        in_specs=[hbm, vmem, vmem, vmem],
        out_specs=(hbm, vmem, vmem),
        scratch_shapes=[
            pltpu.VMEM((rows, 3 * w), BF16),
            pltpu.VMEM((rows, w), BF16),
            pltpu.SemaphoreType.DMA((4,)),
        ],
        cost_estimate=pl.CostEstimate(
            flops=w, bytes_accessed=w, transcendentals=0
        ),
        name="edge",
    )(strip, inverses, *in_vmem(ones, second_edge))


def trailing_far(strip, begun, far, factors, factor_at_two, swap):
    rows = strip.shape[0]
    w = factor_at_two.shape[0]
    half = far.shape[1] // 2
    vmem, hbm = pl.BlockSpec(memory_space=pltpu.VMEM), pl.BlockSpec(memory_space=pl.ANY)
    return pl.pallas_call(
        lambda *refs: far_kernel(w, swap, *refs),
        out_shape=jax.ShapeDtypeStruct(begun.shape, BF16),
        in_specs=[hbm] * 2 + [vmem] * 4,
        out_specs=hbm,
        input_output_aliases={1: 0},
        scratch_shapes=[
            pltpu.VMEM((rows, half), BF16),
            pltpu.VMEM((rows, half), BF16),
            pltpu.SemaphoreType.DMA((2, half // w)),
        ],
        cost_estimate=pl.CostEstimate(
            flops=w, bytes_accessed=w, transcendentals=0
        ),
        name="far_swapped" if swap else "far",
    )(strip, begun, *in_vmem(far, *factors, factor_at_two))


def after(x, gate):
    return lax.optimization_barrier((x, gate))[0]


def body(panel_strip, pivot_inverses, coupling, pivot_nodes):
    strip = panel_strip[0]
    inverses = pivot_inverses[0]
    span = coupling[0]
    w = span.shape[0]
    blocks = lax.axis_size("blk")
    per = w // blocks

    back_near, back_far = (core_passed(span, by) for by in ((1, 2), (None, 3)))

    near_here, far_here = picked_rows(pivot_nodes, strip, w, per)
    near = lax.all_gather(near_here, "blk", axis=0, tiled=True)
    near, far_here = lax.optimization_barrier((near, far_here))
    own = lax.all_to_all(far_here, "blk", 0, 0, tiled=True)
    boundary, factor_at_two, second_edge, one_rows = boundary_of(near, inverses)
    back_near, back_far, boundary = lax.optimization_barrier((back_near, back_far, boundary))

    def advance(current, incoming, reach):
        return matmul_high(matmul_high(reach, incoming.astype(F32)), reach.T) + current

    core_pairs = [[i, i + 1] for i in range(0, blocks, 2)]

    def joined(half):
        return lax.all_gather(half, "blk", axis=1, tiled=True, axis_index_groups=core_pairs)

    arriving = [core_passed(boundary, by) for by in ((1, 3), (2, None))]
    core = lax.axis_index("blk") % 2

    def by_core(zero, one):
        return with_layout_constraint(jnp.where(core == 0, zero, one), Layout((0, 1)))

    pair = matmul_high(by_core(span, back_near), by_core(back_near, back_far))
    pair = lax.all_gather(pair, "blk", axis_index_groups=core_pairs)
    span_two = pair[0]
    span_four = matmul_high(span_two, pair[1])
    reaches = by_core(span, matmul_high(span_two, back_near)), span_two
    half_four = lax.dynamic_slice_in_dim(span_four, core * (w // 2), w // 2, 1)
    half_eight = matmul_high(span_four, passed_along(half_four, "tm", 4))
    terms = jnp.zeros((w, w), F32)
    for incoming, reach in zip(arriving, reaches):
        terms = advance(terms, incoming, reach)
    terms = lax.all_gather(terms, "blk", axis_index_groups=core_pairs)
    current = boundary.astype(F32) + (terms[0] + terms[1])
    wire = current.astype(BF16)

    incoming = passed_along(wire, "tm", 4)
    begun, *factors = trailing_edge(strip, inverses, after(one_rows, wire), second_edge)
    passed_eight = passed_along(half_eight, "tm", 8)
    incoming, begun, half_eight = lax.optimization_barrier((incoming, begun, half_eight))
    current = advance(current, incoming, span_four)
    wire = current.astype(BF16)

    incoming = passed_along(wire, "tm", 8)
    own = after(own, wire)
    other = lax.ppermute(own, "blk", [(i, i ^ 1) for i in range(blocks)])
    trailing = trailing_far(strip, begun, own, factors, factor_at_two, False)
    span_eight = joined(after(half_eight, wire))
    half_sixteen = matmul_high(span_eight, passed_eight)
    incoming, half_sixteen, trailing = lax.optimization_barrier((incoming, half_sixteen, trailing))
    span_sixteen = joined(half_sixteen)
    current = advance(current, incoming, span_eight)
    wire = current.astype(BF16)

    incoming = passed_along(wire, "tm", 16)
    trailing = trailing_far(strip, trailing, other, factors, factor_at_two, True)
    incoming, trailing = lax.optimization_barrier((incoming, trailing))
    current = advance(current, incoming, span_sixteen)
    return (trailing[None], current[None])


def solution(mesh):
    placed = (P("tm", "blk", None), P("tm", None, None, None), P("tm", None, None), P())
    return jax.shard_map(
        body,
        mesh=mesh,
        in_specs=placed,
        out_specs=(P("tm", "blk", None), P("tm", None, None)),
        check_vma=False,
    )
```

```python
import jax
import jax.numpy as jnp
from jax import lax
from jax.experimental.layout import Layout, with_layout_constraint
from jax.experimental import pallas as pl
from jax.experimental.pallas import tpu as pltpu
from jax.sharding import PartitionSpec as P

BF16 = jnp.bfloat16
F32 = jnp.float32
VMEM_BYTES = 16 << 20


def passed_along(x, axis, by):
    count = lax.axis_size(axis)
    return lax.ppermute(x, axis, [(i, i + by) for i in range(count - by)])


def core_passed(x, reaches):
    count, blocks = lax.axis_size("tm"), lax.axis_size("blk")
    pairs = [
        (i * blocks + j, (i + reaches[j % 2]) * blocks + j)
        for i in range(count)
        for j in range(blocks)
        if reaches[j % 2] and i + reaches[j % 2] < count
    ]
    return lax.ppermute(x, ("tm", "blk"), pairs)


def matmul_high(left, right):
    return jnp.dot(left, right, precision=lax.Precision.HIGHEST, preferred_element_type=F32)


def rounded_dot(left, right):
    return jnp.dot(left, right, preferred_element_type=F32).astype(BF16)


def reduced_by(block, factor, rows):
    product = jnp.dot(factor, rows, preferred_element_type=F32)
    return (block.astype(F32) - product).astype(BF16)


def pick_kernel(w, per, chunks, nodes_hbm, strip_hbm, near_ref, far_hbm, strip_ref, nodes_ref, far_ref, sems, far_sems):
    rows = strip_ref.shape[0]
    cols = strip_ref.shape[1] // chunks

    def part(i):
        at = pl.ds(i * cols, cols)
        return pltpu.make_async_copy(strip_hbm.at[:, at], strip_ref.at[:, at], sems.at[i])

    nodes = pltpu.make_async_copy(nodes_hbm, nodes_ref, sems.at[chunks])
    nodes.start()
    for i in [*range(1, chunks), 0]:
        part(i).start()
    nodes.wait()
    me = lax.axis_index("blk")
    lanes = 128
    at_row = lax.broadcasted_iota(jnp.int32, (3 * per, lanes), 0)
    at_lane = lax.broadcasted_iota(jnp.int32, (3 * per, lanes), 1)
    wanted = jnp.zeros((3 * per, lanes), jnp.int32)
    for k in range(3):
        for i in range(per):
            wanted = jnp.where(at_row == k * per + i, nodes_ref[k, me * per + i] - me * rows, wanted)
    picker = jnp.concatenate(
        [(wanted == at_lane + first).astype(F32).astype(BF16) for first in range(0, rows, lanes)], 1
    )
    width = far_ref.shape[2] // 2
    copies = []
    for i in [*range(1, chunks), 0]:
        part(i).wait()
        at = pl.ds(i * cols, cols)
        got = jnp.dot(picker, strip_ref[:, at], preferred_element_type=F32).astype(BF16)
        one, two, edge = got[:per], got[per:2 * per], got[2 * per:]
        if i == 0:
            near_ref[:, :2 * w] = one[:, w:]
            near_ref[:, 2 * w:3 * w] = two[:, :w]
            near_ref[:, 3 * w:4 * w] = two[:, 2 * w:]
            near_ref[:, 4 * w:] = edge
        else:
            far_ref[i - 1, :, :width] = one
            far_ref[i - 1, :, width:] = two
            for row in range((i - 1) * per, far_hbm.shape[0], 2 * per):
                copies.append(
                    pltpu.make_async_copy(
                        far_ref.at[i - 1], far_hbm.at[pl.ds(row, per), :], far_sems.at[row // per]
                    )
                )
                copies[-1].start()
    for copy in copies:
        copy.wait()


def picked_rows(pivot_nodes, strip, w, per):
    rows, width = strip.shape
    chunks = width // (3 * w)
    return pl.pallas_call(
        lambda *refs: pick_kernel(w, per, chunks, *refs),
        out_shape=(
            pltpu.VMEM((per, 7 * w), BF16),
            jax.ShapeDtypeStruct((w, width - 3 * w), BF16),
        ),
        in_specs=[pl.BlockSpec(memory_space=pltpu.HBM), pl.BlockSpec(memory_space=pltpu.HBM)],
        out_specs=(pl.BlockSpec(memory_space=pltpu.VMEM), pl.BlockSpec(memory_space=pl.ANY)),
        scratch_shapes=[
            pltpu.VMEM((rows, width), BF16),
            pltpu.SMEM(pivot_nodes.shape, jnp.int32),
            pltpu.VMEM((chunks - 1, per, width - 3 * w), BF16),
            pltpu.SemaphoreType.DMA((chunks + 1,)),
            pltpu.SemaphoreType.DMA((w // per,)),
        ],
        cost_estimate=pl.CostEstimate(
            flops=2 * 3 * per * rows * width, bytes_accessed=2 * rows * width, transcendentals=0
        ),
        name="pick",
    )(pivot_nodes, strip)


def boundary_kernel(w, near_ref, inverse_ref, boundary_ref, factor_ref, second_ref, ones_ref):
    near = near_ref[...]
    one_edge = near[:, w:2 * w]
    edge = near[:, 4 * w:]
    factor_at_two = rounded_dot(near[:, 2 * w:3 * w], inverse_ref[0])
    factor_at_edge = rounded_dot(edge[:, :w], inverse_ref[0])
    updated = reduced_by(edge[:, w:], factor_at_edge, near[:, :2 * w])
    second_edge = reduced_by(near[:, 3 * w:4 * w], factor_at_two, one_edge)
    factor_two = rounded_dot(updated[:, :w], inverse_ref[1])
    boundary_ref[...] = reduced_by(updated[:, w:], factor_two, second_edge)
    factor_ref[...] = factor_at_two
    second_ref[...] = second_edge
    ones_ref[...] = near[:, :2 * w]


def boundary_of(near, inverses):
    w = near.shape[0]
    block = pltpu.VMEM((w, w), BF16)
    near = pltpu.with_memory_space_constraint(near, pltpu.VMEM)
    vmem = pl.BlockSpec(memory_space=pltpu.VMEM)
    return pl.pallas_call(
        lambda *refs: boundary_kernel(w, *refs),
        out_shape=(block, block, block, pltpu.VMEM((w, 2 * w), BF16)),
        in_specs=[vmem, vmem],
        out_specs=(vmem, vmem, vmem, vmem),
        cost_estimate=pl.CostEstimate(flops=14 * w * w * w, bytes_accessed=12 * w * 2 * w, transcendentals=0),
        compiler_params=pltpu.CompilerParams(vmem_limit_bytes=VMEM_BYTES),
        name="boundary",
    )(near, inverses)


def edge_kernel(
    w, strip_hbm, inverse_ref, ones_ref, second_ref, out_hbm, one_ref, two_ref, strip_ref, edge_ref, sems
):
    def part(i):
        at = pl.ds(i * w, w)
        return pltpu.make_async_copy(strip_hbm.at[:, at], strip_ref.at[:, at], sems.at[i])

    for i in range(3):
        part(i).start()
    part(0).wait()
    one_ref[...] = rounded_dot(strip_ref[:, :w], inverse_ref[0])
    part(1).wait()
    panel = reduced_by(strip_ref[:, w:2 * w], one_ref[...], ones_ref[:, :w])
    two_ref[...] = rounded_dot(panel, inverse_ref[1])
    part(2).wait()
    updated = reduced_by(strip_ref[:, 2 * w:], one_ref[...], ones_ref[:, w:])
    edge_ref[...] = reduced_by(updated, two_ref[...], second_ref[...])
    done = pltpu.make_async_copy(edge_ref, out_hbm.at[:, pl.ds(0, w)], sems.at[3])
    done.start()
    done.wait()


def far_kernel(
    w, swap, strip_hbm, begun_hbm, far_ref, one_ref, two_ref, factor_ref, out_hbm, strip_ref, out_ref, sems
):
    del begun_hbm
    half = far_ref.shape[1] // 2
    count = half // w
    core = lax.rem(lax.axis_index("blk"), 2)
    which = 1 - core if swap else core

    def columns(block):
        return pl.ds(pl.multiple_of((which * count + block) * w, w), w)

    def part(i):
        at = columns(i + 3)
        return pltpu.make_async_copy(strip_hbm.at[:, at], strip_ref.at[:, i * w:(i + 1) * w], sems.at[0, i])

    def done_part(i):
        at = columns(i + 1)
        return pltpu.make_async_copy(out_ref.at[:, i * w:(i + 1) * w], out_hbm.at[:, at], sems.at[1, i])

    for i in range(count):
        part(i).start()
    for i in range(count):
        one_rows = far_ref[:, i * w:(i + 1) * w]
        two_rows = reduced_by(far_ref[:, half + i * w:half + (i + 1) * w], factor_ref[...], one_rows)
        part(i).wait()
        updated = reduced_by(strip_ref[:, i * w:(i + 1) * w], one_ref[...], one_rows)
        out_ref[:, i * w:(i + 1) * w] = reduced_by(updated, two_ref[...], two_rows)
        done_part(i).start()
    for i in range(count):
        done_part(i).wait()


def in_vmem(*arrays):
    return tuple(pltpu.with_memory_space_constraint(x, pltpu.VMEM) for x in arrays)


def trailing_edge(strip, inverses, ones, second_edge):
    rows, width = strip.shape
    w = ones.shape[0]
    vmem, hbm = pl.BlockSpec(memory_space=pltpu.VMEM), pl.BlockSpec(memory_space=pl.ANY)
    return pl.pallas_call(
        lambda *refs: edge_kernel(w, *refs),
        out_shape=(
            jax.ShapeDtypeStruct((rows, width - 2 * w), BF16),
            pltpu.VMEM((rows, w), BF16),
            pltpu.VMEM((rows, w), BF16),
        ),
        in_specs=[hbm, vmem, vmem, vmem],
        out_specs=(hbm, vmem, vmem),
        scratch_shapes=[
            pltpu.VMEM((rows, 3 * w), BF16),
            pltpu.VMEM((rows, w), BF16),
            pltpu.SemaphoreType.DMA((4,)),
        ],
        cost_estimate=pl.CostEstimate(
            flops=w, bytes_accessed=w, transcendentals=0
        ),
        name="edge",
    )(strip, inverses, *in_vmem(ones, second_edge))


def trailing_far(strip, begun, far, factors, factor_at_two, swap):
    rows = strip.shape[0]
    w = factor_at_two.shape[0]
    half = far.shape[1] // 2
    vmem, hbm = pl.BlockSpec(memory_space=pltpu.VMEM), pl.BlockSpec(memory_space=pl.ANY)
    return pl.pallas_call(
        lambda *refs: far_kernel(w, swap, *refs),
        out_shape=jax.ShapeDtypeStruct(begun.shape, BF16),
        in_specs=[hbm] * 2 + [vmem] * 4,
        out_specs=hbm,
        input_output_aliases={1: 0},
        scratch_shapes=[
            pltpu.VMEM((rows, half), BF16),
            pltpu.VMEM((rows, half), BF16),
            pltpu.SemaphoreType.DMA((2, half // w)),
        ],
        cost_estimate=pl.CostEstimate(
            flops=w, bytes_accessed=w, transcendentals=0
        ),
        name="far_swapped" if swap else "far",
    )(strip, begun, *in_vmem(far, *factors, factor_at_two))


def after(x, gate):
    return lax.optimization_barrier((x, gate))[0]


def body(panel_strip, pivot_inverses, coupling, pivot_nodes):
    strip = panel_strip[0]
    inverses = pivot_inverses[0]
    span = coupling[0]
    w = span.shape[0]
    blocks = lax.axis_size("blk")
    per = w // blocks

    back_near, back_far = (core_passed(span, by) for by in ((1, 2), (None, 3)))

    near_here, far_here = picked_rows(pivot_nodes, strip, w, per)
    own = lax.all_to_all(far_here, "blk", 0, 0, tiled=True)
    near = lax.all_gather(near_here, "blk", axis=0, tiled=True)
    boundary, factor_at_two, second_edge, one_rows = boundary_of(near, inverses)
    back_near, back_far, boundary = lax.optimization_barrier((back_near, back_far, boundary))

    def advance(current, incoming, reach):
        return matmul_high(matmul_high(reach, incoming.astype(F32)), reach.T) + current

    core_pairs = [[i, i + 1] for i in range(0, blocks, 2)]

    def joined(half):
        return lax.all_gather(half, "blk", axis=1, tiled=True, axis_index_groups=core_pairs)

    arriving = [core_passed(boundary, by) for by in ((1, 3), (2, None))]
    core = lax.axis_index("blk") % 2

    def by_core(zero, one):
        return with_layout_constraint(jnp.where(core == 0, zero, one), Layout((0, 1)))

    pair = matmul_high(by_core(span, back_near), by_core(back_near, back_far))
    pair = lax.all_gather(pair, "blk", axis_index_groups=core_pairs)
    span_two = pair[0]
    span_four = matmul_high(span_two, pair[1])
    reaches = by_core(span, matmul_high(span_two, back_near)), span_two
    half_four = lax.dynamic_slice_in_dim(span_four, core * (w // 2), w // 2, 1)
    half_eight = matmul_high(span_four, passed_along(half_four, "tm", 4))
    terms = jnp.zeros((w, w), F32)
    for incoming, reach in zip(arriving, reaches):
        terms = advance(terms, incoming, reach)
    terms = lax.all_gather(terms, "blk", axis_index_groups=core_pairs)
    current = boundary.astype(F32) + (terms[0] + terms[1])
    wire = current.astype(BF16)

    incoming = passed_along(wire, "tm", 4)
    begun, *factors = trailing_edge(strip, inverses, after(one_rows, wire), second_edge)
    passed_eight = passed_along(half_eight, "tm", 8)
    incoming, begun, half_eight = lax.optimization_barrier((incoming, begun, half_eight))
    current = advance(current, incoming, span_four)
    wire = current.astype(BF16)

    incoming = passed_along(wire, "tm", 8)
    own = after(own, wire)
    other = lax.ppermute(own, "blk", [(i, i ^ 1) for i in range(blocks)])
    trailing = trailing_far(strip, begun, own, factors, factor_at_two, False)
    span_eight = joined(after(half_eight, wire))
    half_sixteen = matmul_high(span_eight, passed_eight)
    incoming, half_sixteen, trailing = lax.optimization_barrier((incoming, half_sixteen, trailing))
    span_sixteen = joined(half_sixteen)
    current = advance(current, incoming, span_eight)
    wire = current.astype(BF16)

    incoming = passed_along(wire, "tm", 16)
    trailing = trailing_far(strip, trailing, other, factors, factor_at_two, True)
    incoming, trailing = lax.optimization_barrier((incoming, trailing))
    current = advance(current, incoming, span_sixteen)
    return (trailing[None], current[None])


def solution(mesh):
    placed = (P("tm", "blk", None), P("tm", None, None, None), P("tm", None, None), P())
    return jax.shard_map(
        body,
        mesh=mesh,
        in_specs=placed,
        out_specs=(P("tm", "blk", None), P("tm", None, None)),
        check_vma=False,
    )
```
